512 devices in a mesh: sub: 8 (over z_lo), gate: 64 (over z_hi, x, y, core).
Axes of the slice: x: 4, y: 4, z: 16 (z_hi: 2, z_lo: 8; z = z_hi * 8 + z_lo), core: 2. Of those that a mesh axis runs over, the one named last changes fastest.
Arguments:
- raw_echo: bfloat16 [2, 4096, 16384], P(None, ('sub', 'gate')), may hold values from -6 to 6
- delays: int32 [4096], P(('sub', 'gate')), may hold values from 0 to 64
Outputs:
- image: bfloat16 [2, 2048, 16384], P(None, 'sub', 'gate')
The draws below stay inside these ranges and needn't reach their ends.
All inputs are finite; a program needn't handle non-finite values.
Results may differ from the reference program's by a relative error of at most 0.009.
Values may be sent and summed in bfloat16 or wider, within the bound.
A program may use at most 64 MiB of HBM per device.

```python
import math
import jax
import jax.numpy as jnp
from jax import lax

RADIX = 128
SAMPLES = 16384
ANGLES = 256
DELAY_MAX = 64
SUB_PULSES = 512
PULSES = 4096
LEVELS = 3
N_SUB = 8


def with_ends(values, rng, smallest, largest):
    dims = values.shape
    spot = [jax.random.randint(jax.random.fold_in(rng, axis), (), 0, dims[axis]) for axis in range(len(dims))]
    values = values.at[tuple(spot)].set(smallest)
    longest = dims.index(max(dims))
    spot[longest] = (spot[longest] + 1) % dims[longest]
    return values.at[tuple(spot)].set(largest)


def block_scale(own_key, dims, shards, least, high):
    gain = 1.0
    for position, parts in shards:
        draws = jax.random.uniform(jax.random.fold_in(jax.random.fold_in(own_key, 6), position), (parts,), jnp.float32, least / len(shards), high / len(shards))
        gain = gain * jnp.repeat(jnp.exp(draws), dims[position] // parts).reshape((-1,) + (1,) * (len(dims) - 1 - position))
    return gain


def scatter_about(stream_key, shape, width, reach, shards=(), kind=jnp.bfloat16):
    drawn = width * jax.random.normal(stream_key, shape, jnp.float32)
    if shards:
        drawn = drawn * block_scale(stream_key, shape, shards, -0.22, 0.18)
    return jnp.clip(drawn, -reach, reach).astype(kind)


def setup_inputs(seed: int = 0) -> dict:
    seeds = jax.random.split(jax.random.key(seed), 3)
    return {
        "raw_echo": scatter_about(seeds[0], (2, PULSES, SAMPLES), 1.0, 6.0, ((1, 512),)),
        "delays": with_ends(jax.random.randint(seeds[1], (PULSES,), 0, DELAY_MAX + 1), jax.random.fold_in(seeds[1], 1), 0, DELAY_MAX).astype(jnp.int32),
    }


TWO_PI = 2.0 * math.pi

def complex_blocks(real_part, imag_part):
    upper = jnp.stack([real_part, -imag_part], axis=1)
    lower = jnp.stack([imag_part, real_part], axis=1)
    return jnp.stack([upper, lower], axis=0).astype(jnp.bfloat16)

def dft_blocks(order):
    counter = jnp.arange(order, dtype=jnp.int32)
    product = counter[:, None] * counter[None, :] % order
    phases = -TWO_PI / order * product.astype(jnp.float32)
    factor = 1.0 / math.sqrt(order)
    return complex_blocks(jnp.cos(phases) * factor, jnp.sin(phases) * factor)

def steer_blocks(beam_count, pulse_count):
    beam_index = jnp.arange(beam_count, dtype=jnp.int32)
    pulse_index = jnp.arange(pulse_count, dtype=jnp.int32)
    modulus = 16 * beam_count
    product = (2 * beam_index[:, None] - beam_count + 1) * (2 * pulse_index[None, :] - pulse_count + 1) % modulus
    phases = -TWO_PI / modulus * product.astype(jnp.float32)
    factor = 1.0 / math.sqrt(pulse_count)
    return complex_blocks(jnp.cos(phases) * factor, jnp.sin(phases) * factor)

def interp_table(beam_count):
    half_count = beam_count // 2
    targets = jnp.arange(beam_count, dtype=jnp.float32)
    sources = jnp.arange(half_count, dtype=jnp.float32)
    distance = targets[:, None] * 0.5 - 0.25 - sources[None, :]
    taper = jnp.where(jnp.abs(distance) < 4.0, 0.5 + 0.5 * jnp.cos(math.pi * distance / 4.0), 0.0)
    return (jnp.sinc(distance) * taper).astype(jnp.bfloat16)

def rotation(center, numerator, depth, gate_pos):
    modulus = ANGLES * 2 ** (depth + 3)
    turns = jnp.mod(center * numerator, modulus).astype(jnp.float32) / modulus
    center_sq = (center * center).astype(jnp.float32)
    near_term = center_sq / (16.0 * (SAMPLES + gate_pos))
    phases = -TWO_PI * turns[:, None] - TWO_PI / (4 * ANGLES) * near_term[None, :]
    factor = 1.0 / math.sqrt(2.0)
    return (jnp.cos(phases) * factor, jnp.sin(phases) * factor)

def range_compress(raw_block, delay_block):
    pulse_count = raw_block.shape[1]
    dft_table = dft_blocks(RADIX).astype(jnp.float32)
    samples_grid = raw_block.reshape(2, pulse_count, RADIX, RADIX).astype(jnp.float32)
    section_one = jnp.einsum('akcn,cpnm->apkm', dft_table, samples_grid)
    counter = jnp.arange(RADIX, dtype=jnp.int32)
    phases = -TWO_PI / SAMPLES * (counter[:, None] * counter[None, :]).astype(jnp.float32)
    cosine = jnp.cos(phases)
    sine_part = jnp.sin(phases)
    twisted = jnp.stack([section_one[0] * cosine - section_one[1] * sine_part, section_one[0] * sine_part + section_one[1] * cosine]).astype(jnp.bfloat16)
    spectrum = jnp.einsum('akcn,cpjn->apkj', dft_table, twisted.astype(jnp.float32))
    spectrum = spectrum.reshape(2, pulse_count, SAMPLES)
    padded = jnp.pad(spectrum, ((0, 0), (0, 0), (0, DELAY_MAX)))

    def shift_row(pulse_row, start):
        return lax.dynamic_slice_in_dim(pulse_row, start, SAMPLES, axis=1)
    shifted = jax.vmap(shift_row, in_axes=(1, 0), out_axes=1)(padded, delay_block)
    return shifted.astype(jnp.bfloat16)

def merge_level(images, depth, gate_pos):
    pairs = images.shape[0] // 2
    half_count = ANGLES // 2
    sectors = 2 ** depth
    columns = images.shape[-1]
    child = images.reshape(pairs, 2, 2, sectors, half_count, columns).astype(jnp.float32)
    moved = jnp.einsum('jh,bkcqhg->bkcqjg', interp_table(ANGLES).astype(jnp.float32), child)
    row_index = jnp.arange(sectors * ANGLES, dtype=jnp.int32)
    numerator = 2 * row_index + 1 - ANGLES * sectors
    offset = SUB_PULSES * 2 ** (depth - 1) // 2
    total_real = jnp.zeros((pairs, sectors, ANGLES, columns), jnp.float32)
    total_imag = jnp.zeros((pairs, sectors, ANGLES, columns), jnp.float32)
    for member in range(2):
        center = jnp.asarray((2 * member - 1) * offset, dtype=jnp.int32)
        cosine, sine_part = rotation(center, numerator, depth, gate_pos)
        cosine = cosine.reshape(sectors, ANGLES, columns)
        sine_part = sine_part.reshape(sectors, ANGLES, columns)
        part_real = moved[:, member, 0]
        part_imag = moved[:, member, 1]
        total_real = total_real + cosine * part_real - sine_part * part_imag
        total_imag = total_imag + sine_part * part_real + cosine * part_imag
    merged = jnp.stack([total_real, total_imag], axis=1)
    return merged.reshape(pairs, 2, sectors * ANGLES, columns).astype(jnp.bfloat16)

def reverse_blocks(values, depth_count):
    columns = values.shape[-1]
    digits = values.reshape((2,) + (2,) * depth_count + (ANGLES, columns))
    axes_order = (0,) + tuple(range(depth_count, 0, -1)) + (depth_count + 1, depth_count + 2)
    return jnp.transpose(digits, axes_order).reshape(2, 2 ** depth_count, ANGLES, columns)

def reference(raw_echo, delays):
    steering = steer_blocks(ANGLES, SUB_PULSES).astype(jnp.float32)

    def one_sub(sub_number):
        raw_block = lax.dynamic_slice_in_dim(raw_echo, sub_number * SUB_PULSES, SUB_PULSES, axis=1)
        delay_block = lax.dynamic_slice_in_dim(delays, sub_number * SUB_PULSES, SUB_PULSES, axis=0)
        compressed = range_compress(raw_block, delay_block)
        return jnp.einsum('akcm,cmg->akg', steering, compressed.astype(jnp.float32)).astype(jnp.bfloat16)
    level_zero = lax.map(one_sub, jnp.arange(N_SUB, dtype=jnp.int32))
    block_count = 8
    block_width = SAMPLES // block_count
    gate_blocks = level_zero.reshape(N_SUB, 2, ANGLES, block_count, block_width).transpose(3, 0, 1, 2, 4)
    starts = jnp.arange(block_count, dtype=jnp.int32) * block_width

    def one_block(inputs):
        images, start = inputs
        gate_pos = (start + jnp.arange(block_width, dtype=jnp.int32)).astype(jnp.float32)
        for depth in range(1, LEVELS + 1):
            images = merge_level(images, depth, gate_pos)
        return images[0]
    merged = lax.map(one_block, (gate_blocks, starts))
    whole_image = merged.transpose(1, 2, 0, 3).reshape(2, ANGLES * N_SUB, SAMPLES)
    return reverse_blocks(whole_image, LEVELS).reshape(2, ANGLES * N_SUB, SAMPLES)
```

```python
import functools
import math

import jax
import jax.numpy as jnp
import ml_dtypes
import numpy as np
from jax import lax
from jax.experimental import pallas as pl
from jax.experimental.pallas import tpu as pltpu
from jax.sharding import PartitionSpec as P

RADIX = 128
SAMPLES = 16384
ANGLES = 256
SUB_PULSES = 512
N_SUB = 8
HALVES = 2
PEERS = 32
RING = HALVES * N_SUB
OWN = 8
BLOCK = 256
WINDOW = 44
ROWS = 2 * WINDOW
STARTS = (0, 26, 60, 84)
TWO_PI = 2.0 * math.pi
MESH = pl.DeviceIdType.MESH


def bf16(values):
    return values.astype(ml_dtypes.bfloat16)


def complex_rows(table):
    return np.block([[table.real, -table.imag], [table.imag, table.real]])


def dft_matrix():
    count = np.arange(RADIX)
    turns = (count[:, None] * count[None, :]) % RADIX
    return bf16(complex_rows(np.exp(-1j * TWO_PI / RADIX * turns) / math.sqrt(RADIX)))


def twiddle_table():
    count = np.arange(RADIX)
    turns = np.exp(-1j * TWO_PI / SAMPLES * (count[:, None] * count[None, :]))
    return np.stack([turns.real, turns.imag]).astype(np.float32)


def steer_matrix():
    beams = np.concatenate(
        [128 * (q // 4) + STARTS[q % 4] + np.arange(WINDOW) for q in range(N_SUB)]
    )
    halves = []
    for half in range(HALVES):
        pulses = half * PEERS * OWN + np.arange(PEERS * OWN)
        turns = ((2 * beams[:, None] - ANGLES + 1) * (2 * pulses[None, :] - SUB_PULSES + 1)) % 4096
        table = np.exp(-1j * TWO_PI / 4096 * turns) / math.sqrt(SUB_PULSES)
        table = table.reshape(N_SUB, WINDOW, PEERS, OWN)
        upper = np.stack([table.real, -table.imag], axis=3)
        lower = np.stack([table.imag, table.real], axis=3)
        halves.append(np.stack([upper, lower], axis=1).reshape(N_SUB * ROWS, PEERS * 2 * OWN))
    return bf16(np.stack(halves))


def interp_matrix():
    distance = np.arange(ANGLES)[:, None] / 2 - 0.25 - np.arange(ANGLES // 2)[None, :]
    taper = np.where(np.abs(distance) < 4.0, 0.5 + 0.5 * np.cos(math.pi * distance / 4.0), 0.0)
    return bf16(np.sinc(distance) * taper).astype(np.float64)


def turned(rows, member):
    sign = 1 - 2 * member
    return np.exp(sign * 1j * TWO_PI * (2 * rows + 1) / 16)[:, None] / math.sqrt(2.0)


def merge_matrices():
    interp = interp_matrix()
    rows = np.arange(ANGLES)
    half = ANGLES // 2
    early = []
    for kind in range(4):
        second = slice(half * (kind % 2), half * (kind % 2) + half)
        first = slice(half * (kind // 2), half * (kind // 2) + half)
        blocks = []
        for late in range(2):
            for soon in range(2):
                two = (turned(rows, late) * interp)[second]
                one = (turned(rows, soon) * interp)[first]
                window = (two @ one)[:, STARTS[kind] : STARTS[kind] + WINDOW]
                blocks.append(complex_rows(window))
        early.append(np.concatenate(blocks, axis=1))
    last = [complex_rows(turned(rows, member) * interp) for member in range(2)]
    return bf16(np.stack(early)), bf16(np.concatenate(last, axis=1))


def swapped_bits(value):
    return value % 2 * 4 + value // 2 % 2 * 2 + value // 4


def kernel(
    delays,
    raw,
    dft,
    twiddle,
    last,
    steer_all,
    early_all,
    image,
    steer,
    early,
    spread,
    packed,
    twisted,
    rolled,
    blocks,
    pulses,
    outgoing,
    incoming,
    table_sem,
    plane_send,
    plane_recv,
    ring_send,
    ring_recv,
):
    sub = lax.axis_index("sub")
    gate = lax.axis_index("gate")
    half = gate // PEERS
    peer = gate % PEERS
    place = half * N_SUB + sub
    sector = swapped_bits(sub)

    barrier = pltpu.get_barrier_semaphore()

    def greet_plane(step, carry):
        other = half * PEERS + (peer + step) % PEERS
        pl.semaphore_signal(barrier, inc=1, device_id={"gate": other}, device_id_type=MESH)
        return carry

    def greet_ring(step, carry):
        spot = (place + step) % RING
        to = {"sub": spot % N_SUB, "gate": spot // N_SUB * PEERS + peer}
        pl.semaphore_signal(barrier, inc=1, device_id=to, device_id_type=MESH)
        return carry

    lax.fori_loop(1, RING, greet_ring, 0)
    lax.fori_loop(1, PEERS, greet_plane, 0)

    load_steer = pltpu.make_async_copy(steer_all.at[half], steer, table_sem.at[0])
    load_steer.start()
    load_early = pltpu.make_async_copy(early_all.at[sector % 4], early, table_sem.at[1])
    load_early.start()

    for part in range(2):
        spread[part] = raw[part].astype(jnp.float32).reshape(RADIX * OWN, RADIX)
    for part in range(2):
        for pulse in range(OWN):
            packed[part * RADIX : (part + 1) * RADIX, pulse * RADIX : (pulse + 1) * RADIX] = spread[
                part, pl.ds(pulse, RADIX, stride=OWN), :
            ].astype(jnp.bfloat16)
    cosine = twiddle[0]
    sine = twiddle[1]
    for pair in range(OWN // 2):
        section = jnp.dot(
            dft[...],
            packed[:, pair * 2 * RADIX : (pair + 1) * 2 * RADIX],
            preferred_element_type=jnp.float32,
        )
        for side in range(2):
            real = section[:RADIX, side * RADIX : (side + 1) * RADIX]
            imag = section[RADIX:, side * RADIX : (side + 1) * RADIX]
            rows = slice((2 * pair + side) * RADIX, (2 * pair + side + 1) * RADIX)
            twisted[rows, :RADIX] = (real * cosine - imag * sine).astype(jnp.bfloat16)
            twisted[rows, RADIX:] = (real * sine + imag * cosine).astype(jnp.bfloat16)
    lane = lax.broadcasted_iota(jnp.int32, (RADIX, RADIX), 1)
    for part in range(2):
        rolled[part, RADIX:, :] = jnp.zeros((8, RADIX), jnp.float32)
    for pair in range(OWN // 2):
        spectrum = lax.dot_general(
            dft[...],
            twisted[pair * 2 * RADIX : (pair + 1) * 2 * RADIX, :],
            (((1,), (1,)), ((), ())),
            preferred_element_type=jnp.float32,
        )
        for side in range(2):
            pulse = 2 * pair + side
            delay = delays[pulse]
            near = lane < RADIX - delay
            for part in range(2):
                own = spectrum[part * RADIX : (part + 1) * RADIX, side * RADIX : (side + 1) * RADIX]
                own = pltpu.roll(own, RADIX - delay, 1)
                rolled[part, :RADIX, :] = own
                after = rolled[part, 1 : RADIX + 1, :]
                spread[part, pl.ds(pulse, RADIX, stride=OWN), :] = jnp.where(near, own, after)
    rows = jnp.concatenate(
        [spread[part].reshape(RADIX, OWN, RADIX) for part in range(2)], axis=1
    ).astype(jnp.bfloat16)
    rows = rows.reshape(HALVES * PEERS, 2, 2 * OWN, RADIX)
    for side in range(2):
        blocks[:, :, :, side * RADIX : (side + 1) * RADIX] = rows[:, side].reshape(
            HALVES, PEERS, 2 * OWN, RADIX
        )

    pl.semaphore_wait(barrier, RING - 1 + PEERS - 1)

    def plane_copy(step):
        other = (peer + step) % PEERS
        return pltpu.make_async_remote_copy(
            src_ref=blocks.at[:, other],
            dst_ref=pulses.at[:, peer],
            send_sem=plane_send.at[step],
            recv_sem=plane_recv.at[step],
            device_id={"gate": half * PEERS + other},
            device_id_type=MESH,
        )

    def plane_start(step, carry):
        plane_copy(step).start()
        return carry

    lax.fori_loop(1, PEERS, plane_start, 0)
    for side in range(HALVES):
        pulses[side, peer] = blocks[side, peer]
    load_steer.wait()
    load_early.wait()

    def plane_wait(step, carry):
        plane_copy(step).wait()
        return carry

    lax.fori_loop(1, PEERS, plane_wait, 0)

    for side in range(HALVES):
        beams = jnp.dot(
            steer[...],
            pulses[side].reshape(PEERS * 2 * OWN, BLOCK),
            preferred_element_type=jnp.float32,
        )
        for q in range(N_SUB):
            window = beams[q * ROWS : (q + 1) * ROWS]
            outgoing[side, q] = jnp.concatenate(
                [window[:, :RADIX], window[:, RADIX:]], axis=0
            ).astype(jnp.bfloat16)

    def ring_copy(step):
        spot = (place + step) % RING
        there = spot % N_SUB
        return pltpu.make_async_remote_copy(
            src_ref=outgoing.at[spot // N_SUB, swapped_bits(there)],
            dst_ref=incoming.at[half, sub],
            send_sem=ring_send.at[step],
            recv_sem=ring_recv.at[step],
            device_id={"sub": there, "gate": spot // N_SUB * PEERS + peer},
            device_id_type=MESH,
        )

    for distance in range(RING // 2, 0, -1):
        ring_copy(distance).start()
        if distance < RING // 2:
            ring_copy(RING - distance).start()
    incoming[half, sub] = outgoing[half, sector]

    position = (
        gate * BLOCK + lax.broadcasted_iota(jnp.int32, (1, BLOCK), 1) + SAMPLES
    ).astype(jnp.float32)
    phase = (-TWO_PI * 84.0) / position
    gate_cos = jnp.cos(phase)
    gate_sin = jnp.sin(phase)

    def ring_wait(step, carry):
        ring_copy(step).wait()
        return carry

    lax.fori_loop(1, RING, ring_wait, 0)

    total = None
    for late in range(2):
        children = []
        for s in range(4 * late, 4 * late + 4):
            both = incoming[0, s].astype(jnp.float32) + incoming[1, s].astype(jnp.float32)
            children.append(
                jnp.concatenate([both[:ROWS], both[ROWS:]], axis=1).astype(jnp.bfloat16)
            )
        level_two = jnp.dot(
            early[...], jnp.concatenate(children, axis=0), preferred_element_type=jnp.float32
        ).astype(jnp.bfloat16)
        made = jnp.dot(
            last[:, late * ANGLES : (late + 1) * ANGLES],
            level_two,
            preferred_element_type=jnp.float32,
        )
        total = made if total is None else total + made
    real = total[:ANGLES]
    imag = total[ANGLES:]
    image[0] = (real * gate_cos - imag * gate_sin).astype(jnp.bfloat16)
    image[1] = (real * gate_sin + imag * gate_cos).astype(jnp.bfloat16)


def per_device(raw_echo, delays):
    raw = raw_echo.reshape(2, OWN, RADIX, RADIX).transpose(0, 2, 1, 3)
    early, last = merge_matrices()
    vmem = pl.BlockSpec(memory_space=pltpu.VMEM)
    hbm = pl.BlockSpec(memory_space=pl.ANY)
    return pl.pallas_call(
        kernel,
        out_shape=jax.ShapeDtypeStruct((2, ANGLES, BLOCK), jnp.bfloat16),
        in_specs=[pl.BlockSpec(memory_space=pltpu.SMEM), vmem, vmem, vmem, vmem, hbm, hbm],
        out_specs=vmem,
        scratch_shapes=[
            pltpu.VMEM((N_SUB * ROWS, PEERS * 2 * OWN), jnp.bfloat16),
            pltpu.VMEM((ANGLES, 4 * ROWS), jnp.bfloat16),
            pltpu.VMEM((2, RADIX * OWN, RADIX), jnp.float32),
            pltpu.VMEM((2 * RADIX, OWN * RADIX), jnp.bfloat16),
            pltpu.VMEM((OWN * RADIX, 2 * RADIX), jnp.bfloat16),
            pltpu.VMEM((2, RADIX + 8, RADIX), jnp.float32),
            pltpu.VMEM((HALVES, PEERS, 2 * OWN, BLOCK), jnp.bfloat16),
            pltpu.VMEM((HALVES, PEERS, 2 * OWN, BLOCK), jnp.bfloat16),
            pltpu.VMEM((HALVES, N_SUB, 2 * ROWS, RADIX), jnp.bfloat16),
            pltpu.VMEM((HALVES, N_SUB, 2 * ROWS, RADIX), jnp.bfloat16),
            pltpu.SemaphoreType.DMA((2,)),
            pltpu.SemaphoreType.DMA((PEERS,)),
            pltpu.SemaphoreType.DMA((PEERS,)),
            pltpu.SemaphoreType.DMA((RING,)),
            pltpu.SemaphoreType.DMA((RING,)),
        ],
        compiler_params=pltpu.CompilerParams(collective_id=0, has_side_effects=True),
        name="image_formation",
    )(
        delays,
        raw,
        jnp.asarray(dft_matrix()),
        jnp.asarray(twiddle_table()),
        jnp.asarray(last),
        jnp.asarray(steer_matrix()),
        jnp.asarray(early),
    )


def solution(mesh):
    placed = (P(None, ("sub", "gate"), None), P(("sub", "gate")))
    return jax.shard_map(
        per_device, mesh=mesh, in_specs=placed, out_specs=P(None, "sub", "gate"), check_vma=False
    )
```

```python
import functools
import math

import jax
import jax.numpy as jnp
import ml_dtypes
import numpy as np
from jax import lax
from jax.experimental import pallas as pl
from jax.experimental.pallas import tpu as pltpu
from jax.sharding import PartitionSpec as P

RADIX = 128
SAMPLES = 16384
ANGLES = 256
SUB_PULSES = 512
N_SUB = 8
HALVES = 2
PEERS = 32
RING = HALVES * N_SUB
OWN = 8
BLOCK = 256
WINDOW = 44
ROWS = 2 * WINDOW
HELD = RADIX // HALVES + 8
STARTS = (0, 26, 60, 84)
TWO_PI = 2.0 * math.pi
MESH = pl.DeviceIdType.MESH


def bf16(values):
    return values.astype(ml_dtypes.bfloat16)


def complex_rows(table):
    return np.block([[table.real, -table.imag], [table.imag, table.real]])


def dft_matrices():
    count = np.arange(RADIX)
    turns = (count[:, None] * count[None, :]) % RADIX
    table = np.exp(-1j * TWO_PI / RADIX * turns) / math.sqrt(RADIX)
    part = RADIX // HALVES
    rows = np.concatenate([table, np.zeros((8, RADIX))])
    halves = []
    for half in range(HALVES):
        own = rows[half * part : half * part + HELD].copy()
        own[part + 1 :] = 0
        halves.append(complex_rows(own))
    return bf16(complex_rows(table)), bf16(np.stack(halves))


def twiddle_table():
    count = np.arange(RADIX)
    turns = np.exp(-1j * TWO_PI / SAMPLES * (count[:, None] * count[None, :]))
    return np.stack([turns.real, turns.imag]).astype(np.float32)


def steer_matrix():
    beams = np.concatenate(
        [128 * (q // 4) + STARTS[q % 4] + np.arange(WINDOW) for q in range(N_SUB)]
    )
    halves = []
    for half in range(HALVES):
        pulses = half * PEERS * OWN + np.arange(PEERS * OWN)
        turns = ((2 * beams[:, None] - ANGLES + 1) * (2 * pulses[None, :] - SUB_PULSES + 1)) % 4096
        table = np.exp(-1j * TWO_PI / 4096 * turns) / math.sqrt(SUB_PULSES)
        table = table.reshape(N_SUB, WINDOW, PEERS, OWN)
        upper = np.stack([table.real, -table.imag], axis=3)
        lower = np.stack([table.imag, table.real], axis=3)
        halves.append(np.stack([upper, lower], axis=1).reshape(N_SUB * ROWS, PEERS * 2 * OWN))
    return bf16(np.stack(halves))


def interp_matrix():
    distance = np.arange(ANGLES)[:, None] / 2 - 0.25 - np.arange(ANGLES // 2)[None, :]
    taper = np.where(np.abs(distance) < 4.0, 0.5 + 0.5 * np.cos(math.pi * distance / 4.0), 0.0)
    return bf16(np.sinc(distance) * taper).astype(np.float64)


def turned(rows, member):
    sign = 1 - 2 * member
    return np.exp(sign * 1j * TWO_PI * (2 * rows + 1) / 16)[:, None] / math.sqrt(2.0)


def merge_matrices():
    interp = interp_matrix()
    rows = np.arange(ANGLES)
    half = ANGLES // 2
    early = []
    for kind in range(4):
        second = slice(half * (kind % 2), half * (kind % 2) + half)
        first = slice(half * (kind // 2), half * (kind // 2) + half)
        blocks = []
        for late in range(2):
            for soon in range(2):
                two = (turned(rows, late) * interp)[second]
                one = (turned(rows, soon) * interp)[first]
                window = (two @ one)[:, STARTS[kind] : STARTS[kind] + WINDOW]
                blocks.append(complex_rows(window))
        early.append(np.concatenate(blocks, axis=1))
    last = [complex_rows(turned(rows, member) * interp) for member in range(2)]
    return bf16(np.stack(early)), bf16(np.concatenate(last, axis=1))


def swapped_bits(value):
    return value % 2 * 4 + value // 2 % 2 * 2 + value // 4


def kernel(
    delays,
    raw,
    dft,
    dft_half,
    twiddle,
    last,
    steer_all,
    early_all,
    image,
    steer,
    early,
    spread,
    packed,
    twisted,
    rolled,
    blocks,
    pulses,
    outgoing,
    incoming,
    ready,
    table_sem,
    plane_send,
    plane_recv,
    ring_send,
    ring_recv,
):
    sub = lax.axis_index("sub")
    gate = lax.axis_index("gate")
    half = gate // PEERS
    peer = gate % PEERS
    place = half * N_SUB + sub
    sector = swapped_bits(sub)

    barrier = pltpu.get_barrier_semaphore()

    def at(spot):
        return {"sub": spot % N_SUB, "gate": spot // N_SUB * PEERS + peer}

    def greet_plane(step, carry):
        other = half * PEERS + (peer + step) % PEERS
        pl.semaphore_signal(barrier, inc=1, device_id={"gate": other}, device_id_type=MESH)
        return carry

    def greet_ring(step, carry):
        spot = (place + step) % RING

        @pl.when(spot > place)
        def _():
            pl.semaphore_signal(barrier, inc=1, device_id=at(spot), device_id_type=MESH)

        return carry

    def answer_ring(step, carry):
        spot = (place + step) % RING

        @pl.when(spot < place)
        def _():
            pl.semaphore_signal(
                ready.at[place], inc=1, device_id=at(spot), device_id_type=MESH
            )

        return carry

    lax.fori_loop(1, PEERS, greet_plane, 0)
    lax.fori_loop(1, RING, greet_ring, 0)

    load_steer = pltpu.make_async_copy(steer_all.at[half], steer, table_sem.at[0])
    load_steer.start()
    load_early = pltpu.make_async_copy(early_all.at[sector % 4], early, table_sem.at[1])
    load_early.start()

    for part in range(2):
        spread[part] = raw[part].astype(jnp.float32).reshape(RADIX * OWN, RADIX)
    for part in range(2):
        for pulse in range(OWN):
            packed[part * RADIX : (part + 1) * RADIX, pulse * RADIX : (pulse + 1) * RADIX] = spread[
                part, pl.ds(pulse, RADIX, stride=OWN), :
            ].astype(jnp.bfloat16)
    cosine = twiddle[0]
    sine = twiddle[1]
    for pair in range(OWN // 2):
        section = jnp.dot(
            dft[...],
            packed[:, pair * 2 * RADIX : (pair + 1) * 2 * RADIX],
            preferred_element_type=jnp.float32,
        )
        for side in range(2):
            real = section[:RADIX, side * RADIX : (side + 1) * RADIX]
            imag = section[RADIX:, side * RADIX : (side + 1) * RADIX]
            rows = slice((2 * pair + side) * RADIX, (2 * pair + side + 1) * RADIX)
            twisted[rows, :RADIX] = (real * cosine - imag * sine).astype(jnp.bfloat16)
            twisted[rows, RADIX:] = (real * sine + imag * cosine).astype(jnp.bfloat16)
    lane = lax.broadcasted_iota(jnp.int32, (RADIX // HALVES, RADIX), 1)

    def range_gates(side):
        count = RADIX // HALVES
        for pair in range(OWN // 2):
            spectrum = lax.dot_general(
                dft_half[side],
                twisted[pair * 2 * RADIX : (pair + 1) * 2 * RADIX, :],
                (((1,), (1,)), ((), ())),
                preferred_element_type=jnp.float32,
            )
            for late in range(2):
                pulse = 2 * pair + late
                delay = delays[pulse]
                near = lane < RADIX - delay
                for part in range(2):
                    own = pltpu.roll(
                        spectrum[
                            part * HELD : (part + 1) * HELD, late * RADIX : (late + 1) * RADIX
                        ],
                        RADIX - delay,
                        1,
                    )
                    rolled[part, :, :] = own
                    after = rolled[part, 1 : count + 1, :]
                    spread[part, pl.ds(pulse, count, stride=OWN), :] = jnp.where(
                        near, own[:count], after
                    )
        rows = jnp.concatenate(
            [spread[part, : count * OWN].reshape(count, OWN, RADIX) for part in range(2)], axis=1
        ).astype(jnp.bfloat16)
        rows = rows.reshape(PEERS, 2, 2 * OWN, RADIX)
        for late in range(2):
            blocks[side, :, :, late * RADIX : (late + 1) * RADIX] = rows[:, late]

    def plane_copy(side, step):
        other = (peer + step) % PEERS
        return pltpu.make_async_remote_copy(
            src_ref=blocks.at[side, other],
            dst_ref=pulses.at[side, peer],
            send_sem=plane_send.at[side, step],
            recv_sem=plane_recv.at[side, step],
            device_id={"gate": half * PEERS + other},
            device_id_type=MESH,
        )

    def plane_starts(side):
        def start(step, carry):
            plane_copy(side, step).start()
            return carry

        lax.fori_loop(1, PEERS, start, 0)
        pulses[side, peer] = blocks[side, peer]

    def plane_waits(side):
        def wait(step, carry):
            plane_copy(side, step).wait()
            return carry

        lax.fori_loop(1, PEERS, wait, 0)

    def beam_sums(side):
        beams = jnp.dot(
            steer[...],
            pulses[side].reshape(PEERS * 2 * OWN, BLOCK),
            preferred_element_type=jnp.float32,
        )
        for q in range(N_SUB):
            window = beams[q * ROWS : (q + 1) * ROWS]
            outgoing[side, q] = jnp.concatenate(
                [window[:, :RADIX], window[:, RADIX:]], axis=0
            ).astype(jnp.bfloat16)

    def ring_copy(step):
        spot = (place + step) % RING
        return pltpu.make_async_remote_copy(
            src_ref=outgoing.at[spot // N_SUB, swapped_bits(spot % N_SUB)],
            dst_ref=incoming.at[half, sub],
            send_sem=ring_send.at[step],
            recv_sem=ring_recv.at[step],
            device_id=at(spot),
            device_id_type=MESH,
        )

    def ring_starts(side):
        def start(turn, carry):
            distance = RING // 2 - (turn + 1) // 2
            step = jnp.where(turn % 2 == 0, RING - distance, distance)
            spot = (place + step) % RING

            @pl.when(spot // N_SUB == side)
            def _():
                @pl.when(spot > place)
                def _():
                    pl.semaphore_wait(ready.at[spot], 1)

                ring_copy(step).start()

            return carry

        lax.fori_loop(0, RING - 1, start, 0)

    range_gates(0)
    pl.semaphore_wait(barrier, PEERS - 1 + place)
    plane_starts(0)
    lax.fori_loop(1, RING, answer_ring, 0)
    range_gates(1)
    plane_starts(1)
    load_steer.wait()
    load_early.wait()
    for side in range(HALVES):
        plane_waits(side)
        beam_sums(side)
        ring_starts(side)
    incoming[half, sub] = outgoing[half, sector]

    position = (
        gate * BLOCK + lax.broadcasted_iota(jnp.int32, (1, BLOCK), 1) + SAMPLES
    ).astype(jnp.float32)
    phase = (-TWO_PI * 84.0) / position
    gate_cos = jnp.cos(phase)
    gate_sin = jnp.sin(phase)

    def ring_wait(step, carry):
        ring_copy(step).wait()
        return carry

    lax.fori_loop(1, RING, ring_wait, 0)

    total = None
    for late in range(2):
        children = []
        for s in range(4 * late, 4 * late + 4):
            both = incoming[0, s].astype(jnp.float32) + incoming[1, s].astype(jnp.float32)
            children.append(
                jnp.concatenate([both[:ROWS], both[ROWS:]], axis=1).astype(jnp.bfloat16)
            )
        level_two = jnp.dot(
            early[...], jnp.concatenate(children, axis=0), preferred_element_type=jnp.float32
        ).astype(jnp.bfloat16)
        made = jnp.dot(
            last[:, late * ANGLES : (late + 1) * ANGLES],
            level_two,
            preferred_element_type=jnp.float32,
        )
        total = made if total is None else total + made
    real = total[:ANGLES]
    imag = total[ANGLES:]
    image[0] = (real * gate_cos - imag * gate_sin).astype(jnp.bfloat16)
    image[1] = (real * gate_sin + imag * gate_cos).astype(jnp.bfloat16)


def per_device(raw_echo, delays):
    raw = raw_echo.reshape(2, OWN, RADIX, RADIX).transpose(0, 2, 1, 3)
    early, last = merge_matrices()
    dft, dft_half = dft_matrices()
    vmem = pl.BlockSpec(memory_space=pltpu.VMEM)
    hbm = pl.BlockSpec(memory_space=pl.ANY)
    return pl.pallas_call(
        kernel,
        out_shape=jax.ShapeDtypeStruct((2, ANGLES, BLOCK), jnp.bfloat16),
        in_specs=[pl.BlockSpec(memory_space=pltpu.SMEM), vmem, vmem, vmem, vmem, vmem, hbm, hbm],
        out_specs=vmem,
        scratch_shapes=[
            pltpu.VMEM((N_SUB * ROWS, PEERS * 2 * OWN), jnp.bfloat16),
            pltpu.VMEM((ANGLES, 4 * ROWS), jnp.bfloat16),
            pltpu.VMEM((2, RADIX * OWN, RADIX), jnp.float32),
            pltpu.VMEM((2 * RADIX, OWN * RADIX), jnp.bfloat16),
            pltpu.VMEM((OWN * RADIX, 2 * RADIX), jnp.bfloat16),
            pltpu.VMEM((2, HELD, RADIX), jnp.float32),
            pltpu.VMEM((HALVES, PEERS, 2 * OWN, BLOCK), jnp.bfloat16),
            pltpu.VMEM((HALVES, PEERS, 2 * OWN, BLOCK), jnp.bfloat16),
            pltpu.VMEM((HALVES, N_SUB, 2 * ROWS, RADIX), jnp.bfloat16),
            pltpu.VMEM((HALVES, N_SUB, 2 * ROWS, RADIX), jnp.bfloat16),
            pltpu.SemaphoreType.REGULAR((RING,)),
            pltpu.SemaphoreType.DMA((2,)),
            pltpu.SemaphoreType.DMA((HALVES, PEERS)),
            pltpu.SemaphoreType.DMA((HALVES, PEERS)),
            pltpu.SemaphoreType.DMA((RING,)),
            pltpu.SemaphoreType.DMA((RING,)),
        ],
        compiler_params=pltpu.CompilerParams(collective_id=0, has_side_effects=True),
        name="image_formation",
    )(
        delays,
        raw,
        jnp.asarray(dft),
        jnp.asarray(dft_half),
        jnp.asarray(twiddle_table()),
        jnp.asarray(last),
        jnp.asarray(steer_matrix()),
        jnp.asarray(early),
    )


def solution(mesh):
    placed = (P(None, ("sub", "gate"), None), P(("sub", "gate")))
    return jax.shard_map(
        per_device, mesh=mesh, in_specs=placed, out_specs=P(None, "sub", "gate"), check_vma=False
    )
```

```python
import functools
import math

import jax
import jax.numpy as jnp
import ml_dtypes
import numpy as np
from jax import lax
from jax.experimental import pallas as pl
from jax.experimental.pallas import tpu as pltpu
from jax.sharding import PartitionSpec as P

RADIX = 128
SAMPLES = 16384
ANGLES = 256
SUB_PULSES = 512
N_SUB = 8
HALVES = 2
PEERS = 32
RING = HALVES * N_SUB
OWN = 8
BLOCK = 256
WINDOW = 42
EDGE_WINDOW = 38
ROWS = 88
TILES = 21
EDGE_TILES = 19
ALL_TILES = N_SUB * (TILES + EDGE_TILES)
HELD = RADIX // HALVES + 8
STARTS = (0, 26, 60, 90)
WIDTHS = (EDGE_WINDOW, WINDOW, WINDOW, EDGE_WINDOW)
TWO_PI = 2.0 * math.pi
MESH = pl.DeviceIdType.MESH


def bf16(values):
    return values.astype(ml_dtypes.bfloat16)


def complex_rows(table):
    return np.block([[table.real, -table.imag], [table.imag, table.real]])


def dft_matrices():
    count = np.arange(RADIX)
    turns = (count[:, None] * count[None, :]) % RADIX
    table = np.exp(-1j * TWO_PI / RADIX * turns) / math.sqrt(RADIX)
    part = RADIX // HALVES
    rows = np.concatenate([table, np.zeros((8, RADIX))])
    halves = []
    for half in range(HALVES):
        own = rows[half * part : half * part + HELD].copy()
        own[part + 1 :] = 0
        halves.append(complex_rows(own))
    return bf16(complex_rows(table)), bf16(np.stack(halves))


def twiddle_table():
    count = np.arange(RADIX)
    turns = np.exp(-1j * TWO_PI / SAMPLES * (count[:, None] * count[None, :]))
    return np.stack([turns.real, turns.imag]).astype(np.float32)


def steer_matrix():
    result = np.zeros((HALVES, N_SUB, ROWS, PEERS * 2 * OWN))
    for half in range(HALVES):
        pulses = half * PEERS * OWN + np.arange(PEERS * OWN)
        for q in range(N_SUB):
            beams = 128 * (q // 4) + STARTS[q % 4] + np.arange(WIDTHS[q % 4])
            turns = (2 * beams[:, None] - ANGLES + 1) * (2 * pulses[None, :] - SUB_PULSES + 1)
            table = np.exp(-1j * TWO_PI / 4096 * (turns % 4096)) / math.sqrt(SUB_PULSES)
            table = table.reshape(-1, PEERS, OWN)
            upper = np.stack([table.real, -table.imag], axis=2)
            lower = np.stack([table.imag, table.real], axis=2)
            rows = np.stack([upper, lower], axis=1).reshape(-1, PEERS * 2 * OWN)
            result[half, q, : len(rows)] = rows
    return bf16(result.reshape(HALVES, N_SUB * ROWS, PEERS * 2 * OWN))


def interp_matrix():
    distance = np.arange(ANGLES)[:, None] / 2 - 0.25 - np.arange(ANGLES // 2)[None, :]
    taper = np.where(np.abs(distance) < 4.0, 0.5 + 0.5 * np.cos(math.pi * distance / 4.0), 0.0)
    return bf16(np.sinc(distance) * taper).astype(np.float64)


def turned(rows, member):
    sign = 1 - 2 * member
    return np.exp(sign * 1j * TWO_PI * (2 * rows + 1) / 16)[:, None] / math.sqrt(2.0)


def merge_matrices():
    interp = interp_matrix()
    rows = np.arange(ANGLES)
    half = ANGLES // 2
    early = []
    for kind in range(4):
        second = slice(half * (kind % 2), half * (kind % 2) + half)
        first = slice(half * (kind // 2), half * (kind // 2) + half)
        blocks = []
        for late in range(2):
            for soon in range(2):
                two = (turned(rows, late) * interp)[second]
                one = (turned(rows, soon) * interp)[first]
                window = (two @ one)[:, STARTS[kind] : STARTS[kind] + WIDTHS[kind]]
                columns = complex_rows(window).reshape(2 * half, 2, -1).transpose(0, 2, 1)
                columns = columns.reshape(2 * half, -1)
                blocks.append(np.pad(columns, ((0, 0), (0, ROWS - columns.shape[1]))))
        early.append(np.concatenate(blocks, axis=1))
    last = [complex_rows(turned(rows, member) * interp) for member in range(2)]
    return bf16(np.stack(early)), bf16(np.concatenate(last, axis=1))


def bits(value):
    return lax.rem(value, 2), lax.rem(lax.div(value, 2), 2), lax.div(value, 4)


def swapped_bits(value):
    low, middle, high = bits(value)
    return low * 4 + middle * 2 + high


def kernel(
    delays,
    raw_in,
    dft_in,
    dft_half_in,
    twiddle_in,
    last_in,
    steer_in,
    early_in,
    image,
    raw,
    dft,
    dft_half,
    twiddle,
    last,
    steer,
    early,
    spread,
    packed,
    twisted,
    rolled,
    blocks,
    pulses,
    outgoing,
    incoming,
    ready,
    table_sem,
    plane_send,
    plane_recv,
    ring_send,
    ring_recv,
):
    sub = lax.axis_index("sub")
    gate = lax.axis_index("gate")
    half = lax.div(gate, PEERS)
    peer = lax.rem(gate, PEERS)
    place = half * N_SUB + sub
    sector = swapped_bits(sub)

    loads = [
        pltpu.make_async_copy(source, target, table_sem.at[i])
        for i, (source, target) in enumerate(
            (
                (raw_in, raw),
                (dft_in, dft),
                (twiddle_in, twiddle),
                (dft_half_in, dft_half),
                (steer_in.at[half], steer),
                (early_in.at[lax.rem(sector, 4)], early),
                (last_in, last),
            )
        )
    ]
    for load in loads:
        load.start()

    barrier = pltpu.get_barrier_semaphore()

    def at(spot):
        return {"sub": lax.rem(spot, N_SUB), "gate": lax.div(spot, N_SUB) * PEERS + peer}

    def greet_plane(step, carry):
        other = half * PEERS + lax.rem(peer + step, PEERS)
        pl.semaphore_signal(barrier, inc=1, device_id={"gate": other}, device_id_type=MESH)
        return carry

    def greet_ring(spot, carry):
        pl.semaphore_signal(barrier, inc=1, device_id=at(spot), device_id_type=MESH)
        return carry

    def answer_ring(spot, carry):
        pl.semaphore_signal(ready.at[place], inc=1, device_id=at(spot), device_id_type=MESH)
        return carry

    lax.fori_loop(1, PEERS, greet_plane, 0)
    lax.fori_loop(place + 1, RING, greet_ring, 0)

    for load in loads[:3]:
        load.wait()

    for part in range(2):
        spread[part] = raw[part].astype(jnp.float32).reshape(RADIX * OWN, RADIX)
    for part in range(2):
        for pulse in range(OWN):
            packed[part * RADIX : (part + 1) * RADIX, pulse * RADIX : (pulse + 1) * RADIX] = spread[
                part, pl.ds(pulse, RADIX, stride=OWN), :
            ].astype(jnp.bfloat16)
    cosine = twiddle[0]
    sine = twiddle[1]
    for pair in range(OWN // 2):
        section = jnp.dot(
            dft[...],
            packed[:, pair * 2 * RADIX : (pair + 1) * 2 * RADIX],
            preferred_element_type=jnp.float32,
        )
        for side in range(2):
            real = section[:RADIX, side * RADIX : (side + 1) * RADIX]
            imag = section[RADIX:, side * RADIX : (side + 1) * RADIX]
            rows = slice((2 * pair + side) * RADIX, (2 * pair + side + 1) * RADIX)
            twisted[rows, :RADIX] = (real * cosine - imag * sine).astype(jnp.bfloat16)
            twisted[rows, RADIX:] = (real * sine + imag * cosine).astype(jnp.bfloat16)
    lane = lax.broadcasted_iota(jnp.int32, (RADIX // HALVES, RADIX), 1)
    upper = lax.broadcasted_iota(jnp.int32, (8, RADIX), 0) < 4

    def range_gates(side):
        count = RADIX // HALVES
        for pair in range(OWN // 2):
            spectrum = lax.dot_general(
                dft_half[side],
                twisted[pair * 2 * RADIX : (pair + 1) * 2 * RADIX, :],
                (((1,), (1,)), ((), ())),
                preferred_element_type=jnp.float32,
            )
            for late in range(2):
                pulse = 2 * pair + late
                delay = delays[pulse]
                near = lane < RADIX - delay
                for part in range(2):
                    own = pltpu.roll(
                        spectrum[
                            part * HELD : (part + 1) * HELD, late * RADIX : (late + 1) * RADIX
                        ],
                        RADIX - delay,
                        1,
                    )
                    rolled[part, :, :] = own
                    after = rolled[part, 1 : count + 1, :]
                    spread[part, pl.ds(pulse, count, stride=OWN), :] = jnp.where(
                        near, own[:count], after
                    )
        rows = jnp.concatenate(
            [spread[part, : count * OWN].reshape(count, OWN, RADIX) for part in range(2)], axis=1
        ).astype(jnp.bfloat16)
        rows = rows.reshape(PEERS, 2, 2 * OWN, RADIX)
        for late in range(2):
            blocks[side, :, :, late * RADIX : (late + 1) * RADIX] = rows[:, late]

    def plane_copy(side, step):
        other = lax.rem(peer + step, PEERS)
        return pltpu.make_async_remote_copy(
            src_ref=blocks.at[side, other],
            dst_ref=pulses.at[side, peer],
            send_sem=plane_send.at[side],
            recv_sem=plane_recv.at[side],
            device_id={"gate": half * PEERS + other},
            device_id_type=MESH,
        )

    def plane_starts(side):
        def start(step, carry):
            plane_copy(side, step).start()
            return carry

        lax.fori_loop(1, PEERS, start, 0)
        pulses[side, peer] = blocks[side, peer]

    def plane_waits(side):
        others = pl.ds(0, PEERS - 1)
        pltpu.make_async_copy(
            blocks.at[side, others], pulses.at[side, others], plane_recv.at[side]
        ).wait()

    def beam_sums(side):
        beams = jnp.dot(
            steer[...],
            pulses[side].reshape(PEERS * 2 * OWN, BLOCK),
            preferred_element_type=jnp.float32,
        )
        for q in range(N_SUB):
            window = beams[q * ROWS : (q + 1) * ROWS].reshape(ROWS // 8, 8, BLOCK)
            shared = WIDTHS[q % 4] // 4
            base = (side * N_SUB + q) * TILES
            for t in range(shared):
                for lanes in range(2):
                    outgoing[base + 2 * t + lanes] = window[
                        t, :, lanes * RADIX : (lanes + 1) * RADIX
                    ].astype(jnp.bfloat16)
            outgoing[base + 2 * shared] = jnp.where(
                upper, window[shared, :, :RADIX], pltpu.roll(window[shared, :, RADIX:], 4, 0)
            ).astype(jnp.bfloat16)

    def ring_copy(spot, tiles):
        there = lax.rem(spot, N_SUB)
        source = (spot - there + swapped_bits(there)) * TILES
        return pltpu.make_async_remote_copy(
            src_ref=outgoing.at[pl.ds(source, tiles)],
            dst_ref=incoming.at[pl.ds(place * TILES, tiles)],
            send_sem=ring_send,
            recv_sem=ring_recv.at[lax.div(sub, 4)],
            device_id=at(spot),
            device_id_type=MESH,
        )

    def own_copy(tiles):
        return pltpu.make_async_copy(
            outgoing.at[pl.ds((half * N_SUB + sector) * TILES, tiles)],
            incoming.at[pl.ds(place * TILES, tiles)],
            ring_recv.at[lax.div(sub, 4)],
        )

    def on_edge(there):
        _, middle, high = bits(there)
        return middle == high

    def by_size(there, act):
        edge = on_edge(there)

        @pl.when(edge)
        def _():
            act(EDGE_TILES)

        @pl.when(jnp.logical_not(edge))
        def _():
            act(TILES)

    def ring_starts(side):
        def start(turn, carry):
            distance = RING // 2 - lax.div(turn + 1, 2)
            step = jnp.where(lax.rem(turn, 2) == 0, RING - distance, distance)
            spot = lax.rem(place + step, RING)

            @pl.when(lax.div(spot, N_SUB) == side)
            def _():
                @pl.when(spot > place)
                def _():
                    pl.semaphore_wait(ready.at[spot], 1)

                by_size(lax.rem(spot, N_SUB), lambda tiles: ring_copy(spot, tiles).start())

            return carry

        lax.fori_loop(0, RING - 1, start, 0)

    loads[3].wait()
    range_gates(0)
    pl.semaphore_wait(barrier, PEERS - 1 + place)
    plane_starts(0)
    lax.fori_loop(0, place, answer_ring, 0)
    range_gates(1)
    plane_starts(1)
    loads[4].wait()
    for side in range(HALVES):
        plane_waits(side)
        beam_sums(side)
        ring_starts(side)
    by_size(sub, lambda tiles: own_copy(tiles).start())
    for load in loads[5:]:
        load.wait()

    position = (
        gate * BLOCK + lax.broadcasted_iota(jnp.int32, (1, BLOCK), 1) + SAMPLES
    ).astype(jnp.float32)
    phase = (-TWO_PI * 84.0) / position
    gate_cos = jnp.cos(phase)
    gate_sin = jnp.sin(phase)

    edge = on_edge(sub)

    def taken(late, tiles):
        count = pl.ds(0, N_SUB * tiles)
        pltpu.make_async_copy(outgoing.at[count], incoming.at[count], ring_recv.at[late]).wait()

    total = None
    for late in range(2):
        by_size(sub, functools.partial(taken, late))
        children = []
        for s in range(4 * late, 4 * late + 4):
            both = [
                incoming[pl.ds((side * N_SUB + s) * TILES, TILES)].astype(jnp.float32)
                for side in range(HALVES)
            ]
            both = both[0] + both[1]
            paired = both[: TILES - 1].reshape(TILES // 2, 2, 8, RADIX)
            lanes = []
            for side in range(2):
                last_tile = both[TILES - 1]
                edge_tile = both[EDGE_TILES - 1]
                if side == 1:
                    last_tile = pltpu.roll(last_tile, 4, 0)
                    edge_tile = pltpu.roll(edge_tile, 4, 0)
                tiles = [
                    paired[: TILES // 2 - 1, side],
                    jnp.where(edge, edge_tile, paired[TILES // 2 - 1, side])[None],
                    jnp.where(edge, 0.0, last_tile)[None],
                ]
                lanes.append(jnp.concatenate(tiles, axis=0).reshape(ROWS, RADIX))
            children.append(jnp.concatenate(lanes, axis=1).astype(jnp.bfloat16))
        level_two = jnp.dot(
            early[...], jnp.concatenate(children, axis=0), preferred_element_type=jnp.float32
        ).astype(jnp.bfloat16)
        made = jnp.dot(
            last[:, late * ANGLES : (late + 1) * ANGLES],
            level_two,
            preferred_element_type=jnp.float32,
        )
        total = made if total is None else total + made
    real = total[:ANGLES]
    imag = total[ANGLES:]
    image[0] = (real * gate_cos - imag * gate_sin).astype(jnp.bfloat16)
    image[1] = (real * gate_sin + imag * gate_cos).astype(jnp.bfloat16)

    for side in range(HALVES):
        others = pl.ds(0, PEERS - 1)
        pltpu.make_async_copy(
            blocks.at[side, others], pulses.at[side, others], plane_send.at[side]
        ).wait()

    def sent(tiles):
        count = pl.ds(0, ALL_TILES - tiles)
        pltpu.make_async_copy(outgoing.at[count], incoming.at[count], ring_send).wait()

    by_size(sub, sent)


def per_device(raw_echo, delays):
    raw = raw_echo.reshape(2, OWN, RADIX, RADIX).transpose(0, 2, 1, 3)
    early, last = merge_matrices()
    dft, dft_half = dft_matrices()
    vmem = pl.BlockSpec(memory_space=pltpu.VMEM)
    hbm = pl.BlockSpec(memory_space=pl.ANY)
    return pl.pallas_call(
        kernel,
        out_shape=jax.ShapeDtypeStruct((2, ANGLES, BLOCK), jnp.bfloat16),
        in_specs=[pl.BlockSpec(memory_space=pltpu.SMEM)] + [hbm] * 7,
        out_specs=vmem,
        scratch_shapes=[
            pltpu.VMEM((2, RADIX, OWN, RADIX), jnp.bfloat16),
            pltpu.VMEM(dft.shape, jnp.bfloat16),
            pltpu.VMEM(dft_half.shape, jnp.bfloat16),
            pltpu.VMEM((2, RADIX, RADIX), jnp.float32),
            pltpu.VMEM(last.shape, jnp.bfloat16),
            pltpu.VMEM((N_SUB * ROWS, PEERS * 2 * OWN), jnp.bfloat16),
            pltpu.VMEM((ANGLES, 4 * ROWS), jnp.bfloat16),
            pltpu.VMEM((2, RADIX * OWN, RADIX), jnp.float32),
            pltpu.VMEM((2 * RADIX, OWN * RADIX), jnp.bfloat16),
            pltpu.VMEM((OWN * RADIX, 2 * RADIX), jnp.bfloat16),
            pltpu.VMEM((2, HELD, RADIX), jnp.float32),
            pltpu.VMEM((HALVES, PEERS, 2 * OWN, BLOCK), jnp.bfloat16),
            pltpu.VMEM((HALVES, PEERS, 2 * OWN, BLOCK), jnp.bfloat16),
            pltpu.VMEM((RING * TILES, 8, RADIX), jnp.bfloat16),
            pltpu.VMEM((RING * TILES, 8, RADIX), jnp.bfloat16),
            pltpu.SemaphoreType.REGULAR((RING,)),
            pltpu.SemaphoreType.DMA((7,)),
            pltpu.SemaphoreType.DMA((HALVES,)),
            pltpu.SemaphoreType.DMA((HALVES,)),
            pltpu.SemaphoreType.DMA,
            pltpu.SemaphoreType.DMA((2,)),
        ],
        compiler_params=pltpu.CompilerParams(collective_id=0, has_side_effects=True),
        name="image_formation",
    )(
        delays,
        raw,
        jnp.asarray(dft),
        jnp.asarray(dft_half),
        jnp.asarray(twiddle_table()),
        jnp.asarray(last),
        jnp.asarray(steer_matrix()),
        jnp.asarray(early),
    )


def solution(mesh):
    placed = (P(None, ("sub", "gate"), None), P(("sub", "gate")))
    return jax.shard_map(
        per_device, mesh=mesh, in_specs=placed, out_specs=P(None, "sub", "gate"), check_vma=False
    )
```

```python
import functools
import math

import jax
import jax.numpy as jnp
import ml_dtypes
import numpy as np
from jax import lax
from jax.experimental import pallas as pl
from jax.experimental.pallas import tpu as pltpu
from jax.sharding import PartitionSpec as P

RADIX = 128
SAMPLES = 16384
ANGLES = 256
SUB_PULSES = 512
N_SUB = 8
HALVES = 2
PEERS = 32
RING = HALVES * N_SUB
OWN = 8
BLOCK = 256
WINDOW = 42
EDGE_WINDOW = 38
ROWS = 88
TILES = 21
EDGE_TILES = 19
FIRST_TILES = 10
ALL_TILES = N_SUB * (TILES + EDGE_TILES)
HELD = RADIX // HALVES + 8
STARTS = (0, 26, 60, 90)
WIDTHS = (EDGE_WINDOW, WINDOW, WINDOW, EDGE_WINDOW)
TWO_PI = 2.0 * math.pi
MESH = pl.DeviceIdType.MESH


def bf16(values):
    return values.astype(ml_dtypes.bfloat16)


def complex_rows(table):
    return np.block([[table.real, -table.imag], [table.imag, table.real]])


def dft_matrices():
    count = np.arange(RADIX)
    turns = (count[:, None] * count[None, :]) % RADIX
    table = np.exp(-1j * TWO_PI / RADIX * turns) / math.sqrt(RADIX)
    part = RADIX // HALVES
    rows = np.concatenate([table, np.zeros((8, RADIX))])
    halves = []
    for half in range(HALVES):
        own = rows[half * part : half * part + HELD].copy()
        own[part + 1 :] = 0
        halves.append(complex_rows(own))
    return bf16(complex_rows(table)), bf16(np.stack(halves))


def twiddle_table():
    count = np.arange(RADIX)
    turns = np.exp(-1j * TWO_PI / SAMPLES * (count[:, None] * count[None, :]))
    return np.stack([turns.real, turns.imag]).astype(np.float32)


def steer_matrix():
    result = np.zeros((HALVES, N_SUB, ROWS, PEERS * 2 * OWN))
    for half in range(HALVES):
        pulses = half * PEERS * OWN + np.arange(PEERS * OWN)
        for q in range(N_SUB):
            beams = 128 * (q // 4) + STARTS[q % 4] + np.arange(WIDTHS[q % 4])
            turns = (2 * beams[:, None] - ANGLES + 1) * (2 * pulses[None, :] - SUB_PULSES + 1)
            table = np.exp(-1j * TWO_PI / 4096 * (turns % 4096)) / math.sqrt(SUB_PULSES)
            table = table.reshape(-1, PEERS, OWN)
            upper = np.stack([table.real, -table.imag], axis=2)
            lower = np.stack([table.imag, table.real], axis=2)
            rows = np.stack([upper, lower], axis=1).reshape(-1, PEERS * 2 * OWN)
            result[half, q, : len(rows)] = rows
    return bf16(result.reshape(HALVES, N_SUB * ROWS, PEERS * 2 * OWN))


def interp_matrix():
    distance = np.arange(ANGLES)[:, None] / 2 - 0.25 - np.arange(ANGLES // 2)[None, :]
    taper = np.where(np.abs(distance) < 4.0, 0.5 + 0.5 * np.cos(math.pi * distance / 4.0), 0.0)
    return bf16(np.sinc(distance) * taper).astype(np.float64)


def turned(rows, member):
    sign = 1 - 2 * member
    return np.exp(sign * 1j * TWO_PI * (2 * rows + 1) / 16)[:, None] / math.sqrt(2.0)


def merge_matrices():
    interp = interp_matrix()
    rows = np.arange(ANGLES)
    half = ANGLES // 2
    early = []
    for kind in range(4):
        second = slice(half * (kind % 2), half * (kind % 2) + half)
        first = slice(half * (kind // 2), half * (kind // 2) + half)
        blocks = []
        for late in range(2):
            for soon in range(2):
                two = (turned(rows, late) * interp)[second]
                one = (turned(rows, soon) * interp)[first]
                window = (two @ one)[:, STARTS[kind] : STARTS[kind] + WIDTHS[kind]]
                columns = complex_rows(window).reshape(2 * half, 2, -1).transpose(0, 2, 1)
                columns = columns.reshape(2 * half, -1)
                blocks.append(np.pad(columns, ((0, 0), (0, ROWS - columns.shape[1]))))
        early.append(np.concatenate(blocks, axis=1))
    last = [complex_rows(turned(rows, member) * interp) for member in range(2)]
    return bf16(np.stack(early)), bf16(np.concatenate(last, axis=1))


def bits(value):
    return lax.rem(value, 2), lax.rem(lax.div(value, 2), 2), lax.div(value, 4)


def swapped_bits(value):
    low, middle, high = bits(value)
    return low * 4 + middle * 2 + high


def kernel(
    delays,
    raw_in,
    dft_in,
    dft_half_in,
    twiddle_in,
    last_in,
    steer_in,
    early_in,
    image,
    raw,
    dft,
    dft_half,
    twiddle,
    last,
    steer,
    early,
    spread,
    packed,
    twisted,
    rolled,
    blocks,
    pulses,
    kept,
    outgoing,
    incoming,
    ready,
    table_sem,
    plane_send,
    plane_recv,
    ring_send,
    ring_recv,
):
    sub = lax.axis_index("sub")
    gate = lax.axis_index("gate")
    half = lax.div(gate, PEERS)
    peer = lax.rem(gate, PEERS)
    place = half * N_SUB + sub
    sector = swapped_bits(sub)

    loads = [
        pltpu.make_async_copy(source, target, table_sem.at[i])
        for i, (source, target) in enumerate(
            (
                (raw_in, raw),
                (dft_in, dft),
                (twiddle_in, twiddle),
                (dft_half_in, dft_half),
                (steer_in.at[half], steer),
                (early_in.at[lax.rem(sector, 4)], early),
                (last_in, last),
            )
        )
    ]
    for load in loads:
        load.start()

    barrier = pltpu.get_barrier_semaphore()

    def at(spot):
        return {"sub": lax.rem(spot, N_SUB), "gate": lax.div(spot, N_SUB) * PEERS + peer}

    def greet_plane(step, carry):
        other = half * PEERS + lax.rem(peer + step, PEERS)
        pl.semaphore_signal(barrier, inc=1, device_id={"gate": other}, device_id_type=MESH)
        return carry

    def greet_ring(spot, carry):
        pl.semaphore_signal(barrier, inc=1, device_id=at(spot), device_id_type=MESH)
        return carry

    def answer_ring(spot, carry):
        pl.semaphore_signal(ready.at[place], inc=1, device_id=at(spot), device_id_type=MESH)
        return carry

    lax.fori_loop(1, PEERS, greet_plane, 0)
    lax.fori_loop(place + 1, RING, greet_ring, 0)

    for load in loads[:3]:
        load.wait()

    for part in range(2):
        spread[part] = raw[part].astype(jnp.float32).reshape(RADIX * OWN, RADIX)
    for part in range(2):
        for pulse in range(OWN):
            packed[part * RADIX : (part + 1) * RADIX, pulse * RADIX : (pulse + 1) * RADIX] = spread[
                part, pl.ds(pulse, RADIX, stride=OWN), :
            ].astype(jnp.bfloat16)
    cosine = twiddle[0]
    sine = twiddle[1]
    for pair in range(OWN // 2):
        section = jnp.dot(
            dft[...],
            packed[:, pair * 2 * RADIX : (pair + 1) * 2 * RADIX],
            preferred_element_type=jnp.float32,
        )
        for side in range(2):
            real = section[:RADIX, side * RADIX : (side + 1) * RADIX]
            imag = section[RADIX:, side * RADIX : (side + 1) * RADIX]
            rows = slice((2 * pair + side) * RADIX, (2 * pair + side + 1) * RADIX)
            twisted[rows, :RADIX] = (real * cosine - imag * sine).astype(jnp.bfloat16)
            twisted[rows, RADIX:] = (real * sine + imag * cosine).astype(jnp.bfloat16)
    lane = lax.broadcasted_iota(jnp.int32, (RADIX // HALVES, RADIX), 1)
    upper = lax.broadcasted_iota(jnp.int32, (8, RADIX), 0) < 4

    def range_gates(side):
        count = RADIX // HALVES
        for pair in range(OWN // 2):
            spectrum = lax.dot_general(
                dft_half[side],
                twisted[pair * 2 * RADIX : (pair + 1) * 2 * RADIX, :],
                (((1,), (1,)), ((), ())),
                preferred_element_type=jnp.float32,
            )
            for late in range(2):
                pulse = 2 * pair + late
                delay = delays[pulse]
                near = lane < RADIX - delay
                for part in range(2):
                    own = pltpu.roll(
                        spectrum[
                            part * HELD : (part + 1) * HELD, late * RADIX : (late + 1) * RADIX
                        ],
                        RADIX - delay,
                        1,
                    )
                    rolled[part, :, :] = own
                    after = rolled[part, 1 : count + 1, :]
                    spread[part, pl.ds(pulse, count, stride=OWN), :] = jnp.where(
                        near, own[:count], after
                    )
        rows = jnp.concatenate(
            [spread[part, : count * OWN].reshape(count, OWN, RADIX) for part in range(2)], axis=1
        ).astype(jnp.bfloat16)
        rows = rows.reshape(PEERS, 2, 2 * OWN, RADIX)
        for late in range(2):
            blocks[late, side] = rows[:, late]

    def plane_copy(chunk, step):
        other = lax.rem(peer + step, PEERS)
        return pltpu.make_async_remote_copy(
            src_ref=blocks.at[chunk, :, other],
            dst_ref=pulses.at[chunk, :, peer],
            send_sem=plane_send.at[chunk],
            recv_sem=plane_recv.at[chunk],
            device_id={"gate": half * PEERS + other},
            device_id_type=MESH,
        )

    def plane_starts(chunk):
        def start(step, carry):
            plane_copy(chunk, step).start()
            return carry

        lax.fori_loop(1, PEERS, start, 0)
        for side in range(HALVES):
            pulses[chunk, side, peer] = blocks[chunk, side, peer]

    def plane_wait(chunk, semaphores):
        others = pl.ds(0, PEERS - 1)
        pltpu.make_async_copy(
            blocks.at[chunk, :, others], pulses.at[chunk, :, others], semaphores.at[chunk]
        ).wait()

    def beam_sums(chunk):
        beams = jnp.dot(
            steer[...],
            jnp.concatenate(
                [pulses[chunk, side].reshape(PEERS * 2 * OWN, RADIX) for side in range(HALVES)],
                axis=1,
            ),
            preferred_element_type=jnp.float32,
        )
        for side in range(HALVES):
            for q in range(N_SUB):
                window = beams[q * ROWS : (q + 1) * ROWS, side * RADIX : (side + 1) * RADIX]
                window = window.reshape(ROWS // 8, 8, RADIX)
                shared = WIDTHS[q % 4] // 4
                slot = side * N_SUB + q
                base = slot * TILES + chunk * FIRST_TILES
                for t in range(shared):
                    outgoing[base + t] = window[t].astype(jnp.bfloat16)
                if chunk == 0:
                    kept[slot] = window[shared]
                else:
                    outgoing[base + shared] = jnp.where(
                        upper, kept[slot], pltpu.roll(window[shared], 4, 0)
                    ).astype(jnp.bfloat16)

    def ring_copy(chunk, spot, tiles):
        there = lax.rem(spot, N_SUB)
        source = (spot - there + swapped_bits(there)) * TILES + chunk * FIRST_TILES
        return pltpu.make_async_remote_copy(
            src_ref=outgoing.at[pl.ds(source, tiles)],
            dst_ref=incoming.at[pl.ds(place * TILES + chunk * FIRST_TILES, tiles)],
            send_sem=ring_send,
            recv_sem=ring_recv.at[lax.div(sub, 4)],
            device_id=at(spot),
            device_id_type=MESH,
        )

    def own_copy(chunk, tiles):
        source = (half * N_SUB + sector) * TILES + chunk * FIRST_TILES
        return pltpu.make_async_copy(
            outgoing.at[pl.ds(source, tiles)],
            incoming.at[pl.ds(place * TILES + chunk * FIRST_TILES, tiles)],
            ring_recv.at[lax.div(sub, 4)],
        )

    def on_edge(there):
        _, middle, high = bits(there)
        return middle == high

    def by_size(there, small, large, act):
        edge = on_edge(there)

        @pl.when(edge)
        def _():
            act(small)

        @pl.when(jnp.logical_not(edge))
        def _():
            act(large)

    def ring_starts(chunk):
        sizes = EDGE_WINDOW // 4 + chunk, WINDOW // 4 + chunk

        def start(spot, carry):
            there = lax.rem(spot, N_SUB)
            by_size(there, *sizes, lambda tiles: ring_copy(chunk, spot, tiles).start())
            return carry

        def start_later(spot, carry):
            if chunk == 0:
                pl.semaphore_wait(ready.at[spot], 1)
            return start(spot, carry)

        lax.fori_loop(0, place, start, 0)
        lax.fori_loop(place + 1, RING, start_later, 0)
        by_size(sub, *sizes, lambda tiles: own_copy(chunk, tiles).start())

    loads[3].wait()
    for side in range(HALVES):
        range_gates(side)
    pl.semaphore_wait(barrier, PEERS - 1 + place)
    plane_starts(0)
    lax.fori_loop(0, place, answer_ring, 0)
    plane_starts(1)
    loads[4].wait()
    for chunk in range(2):
        plane_wait(chunk, plane_recv)
        beam_sums(chunk)
        ring_starts(chunk)
    for load in loads[5:]:
        load.wait()

    position = (
        gate * BLOCK + lax.broadcasted_iota(jnp.int32, (1, BLOCK), 1) + SAMPLES
    ).astype(jnp.float32)
    phase = (-TWO_PI * 84.0) / position
    gate_cos = jnp.cos(phase)
    gate_sin = jnp.sin(phase)

    edge = on_edge(sub)

    def taken(late, tiles):
        count = pl.ds(0, N_SUB * tiles)
        pltpu.make_async_copy(outgoing.at[count], incoming.at[count], ring_recv.at[late]).wait()

    total = None
    for late in range(2):
        by_size(sub, EDGE_TILES, TILES, functools.partial(taken, late))
        children = []
        for s in range(4 * late, 4 * late + 4):
            both = [
                incoming[pl.ds((side * N_SUB + s) * TILES, TILES)].astype(jnp.float32)
                for side in range(HALVES)
            ]
            both = both[0] + both[1]
            lanes = []
            for chunk in range(2):
                ends = [both[EDGE_TILES], both[TILES - 1]]
                if chunk == 1:
                    ends = [pltpu.roll(end, 4, 0) for end in ends]
                first = chunk * FIRST_TILES
                tiles = [
                    both[first : first + FIRST_TILES - 1],
                    jnp.where(edge, ends[0], both[first + FIRST_TILES - 1])[None],
                    jnp.where(edge, 0.0, ends[1])[None],
                ]
                lanes.append(jnp.concatenate(tiles, axis=0).reshape(ROWS, RADIX))
            children.append(jnp.concatenate(lanes, axis=1).astype(jnp.bfloat16))
        level_two = jnp.dot(
            early[...], jnp.concatenate(children, axis=0), preferred_element_type=jnp.float32
        ).astype(jnp.bfloat16)
        made = jnp.dot(
            last[:, late * ANGLES : (late + 1) * ANGLES],
            level_two,
            preferred_element_type=jnp.float32,
        )
        total = made if total is None else total + made
    real = total[:ANGLES]
    imag = total[ANGLES:]
    image[0] = (real * gate_cos - imag * gate_sin).astype(jnp.bfloat16)
    image[1] = (real * gate_sin + imag * gate_cos).astype(jnp.bfloat16)

    for chunk in range(2):
        plane_wait(chunk, plane_send)

    def sent(tiles):
        count = pl.ds(0, ALL_TILES - tiles)
        pltpu.make_async_copy(outgoing.at[count], incoming.at[count], ring_send).wait()

    by_size(sub, EDGE_TILES, TILES, sent)


def per_device(raw_echo, delays):
    raw = raw_echo.reshape(2, OWN, RADIX, RADIX).transpose(0, 2, 1, 3)
    early, last = merge_matrices()
    dft, dft_half = dft_matrices()
    vmem = pl.BlockSpec(memory_space=pltpu.VMEM)
    hbm = pl.BlockSpec(memory_space=pl.ANY)
    return pl.pallas_call(
        kernel,
        out_shape=pltpu.VMEM((2, ANGLES, BLOCK), jnp.bfloat16),
        in_specs=[pl.BlockSpec(memory_space=pltpu.SMEM)] + [hbm] * 7,
        out_specs=vmem,
        scratch_shapes=[
            pltpu.VMEM((2, RADIX, OWN, RADIX), jnp.bfloat16),
            pltpu.VMEM(dft.shape, jnp.bfloat16),
            pltpu.VMEM(dft_half.shape, jnp.bfloat16),
            pltpu.VMEM((2, RADIX, RADIX), jnp.float32),
            pltpu.VMEM(last.shape, jnp.bfloat16),
            pltpu.VMEM((N_SUB * ROWS, PEERS * 2 * OWN), jnp.bfloat16),
            pltpu.VMEM((ANGLES, 4 * ROWS), jnp.bfloat16),
            pltpu.VMEM((2, RADIX * OWN, RADIX), jnp.float32),
            pltpu.VMEM((2 * RADIX, OWN * RADIX), jnp.bfloat16),
            pltpu.VMEM((OWN * RADIX, 2 * RADIX), jnp.bfloat16),
            pltpu.VMEM((2, HELD, RADIX), jnp.float32),
            pltpu.VMEM((2, HALVES, PEERS, 2 * OWN, RADIX), jnp.bfloat16),
            pltpu.VMEM((2, HALVES, PEERS, 2 * OWN, RADIX), jnp.bfloat16),
            pltpu.VMEM((RING, 8, RADIX), jnp.float32),
            pltpu.VMEM((RING * TILES, 8, RADIX), jnp.bfloat16),
            pltpu.VMEM((RING * TILES, 8, RADIX), jnp.bfloat16),
            pltpu.SemaphoreType.REGULAR((RING,)),
            pltpu.SemaphoreType.DMA((7,)),
            pltpu.SemaphoreType.DMA((HALVES,)),
            pltpu.SemaphoreType.DMA((HALVES,)),
            pltpu.SemaphoreType.DMA,
            pltpu.SemaphoreType.DMA((2,)),
        ],
        compiler_params=pltpu.CompilerParams(collective_id=0, has_side_effects=True),
        name="image_formation",
    )(
        delays,
        raw,
        jnp.asarray(dft),
        jnp.asarray(dft_half),
        jnp.asarray(twiddle_table()),
        jnp.asarray(last),
        jnp.asarray(steer_matrix()),
        jnp.asarray(early),
    )


def solution(mesh):
    placed = (P(None, ("sub", "gate"), None), P(("sub", "gate")))
    return jax.shard_map(
        per_device, mesh=mesh, in_specs=placed, out_specs=P(None, "sub", "gate"), check_vma=False
    )
```

```python
import functools
import math

import jax
import jax.numpy as jnp
import ml_dtypes
import numpy as np
from jax import lax
from jax.experimental import pallas as pl
from jax.experimental.pallas import tpu as pltpu
from jax.sharding import PartitionSpec as P

RADIX = 128
SAMPLES = 16384
ANGLES = 256
SUB_PULSES = 512
N_SUB = 8
HALVES = 2
PEERS = 32
RING = HALVES * N_SUB
OWN = 8
BLOCK = 256
WINDOW = 42
EDGE_WINDOW = 38
ROWS = 88
TILES = 21
EDGE_TILES = 19
ALL_TILES = N_SUB * (TILES + EDGE_TILES)
HELD = RADIX // HALVES + 8
STARTS = (0, 26, 60, 90)
WIDTHS = (EDGE_WINDOW, WINDOW, WINDOW, EDGE_WINDOW)
TWO_PI = 2.0 * math.pi
MESH = pl.DeviceIdType.MESH


def bf16(values):
    return values.astype(ml_dtypes.bfloat16)


def complex_rows(table):
    return np.block([[table.real, -table.imag], [table.imag, table.real]])


def dft_matrices():
    count = np.arange(RADIX)
    turns = (count[:, None] * count[None, :]) % RADIX
    table = np.exp(-1j * TWO_PI / RADIX * turns) / math.sqrt(RADIX)
    part = RADIX // HALVES
    rows = np.concatenate([table, np.zeros((8, RADIX))])
    halves = []
    for half in range(HALVES):
        own = rows[half * part : half * part + HELD].copy()
        own[part + 1 :] = 0
        halves.append(complex_rows(own))
    return bf16(complex_rows(table)), bf16(np.stack(halves))


def twiddle_table():
    count = np.arange(RADIX)
    turns = np.exp(-1j * TWO_PI / SAMPLES * (count[:, None] * count[None, :]))
    return np.stack([turns.real, turns.imag]).astype(np.float32)


def steer_matrix():
    result = np.zeros((HALVES, N_SUB, ROWS, PEERS * 2 * OWN))
    for half in range(HALVES):
        pulses = half * PEERS * OWN + np.arange(PEERS * OWN)
        for q in range(N_SUB):
            beams = 128 * (q // 4) + STARTS[q % 4] + np.arange(WIDTHS[q % 4])
            turns = (2 * beams[:, None] - ANGLES + 1) * (2 * pulses[None, :] - SUB_PULSES + 1)
            table = np.exp(-1j * TWO_PI / 4096 * (turns % 4096)) / math.sqrt(SUB_PULSES)
            table = table.reshape(-1, PEERS, OWN)
            upper = np.stack([table.real, -table.imag], axis=2)
            lower = np.stack([table.imag, table.real], axis=2)
            rows = np.stack([upper, lower], axis=1).reshape(-1, PEERS * 2 * OWN)
            result[half, q, : len(rows)] = rows
    return bf16(result.reshape(HALVES, N_SUB * ROWS, PEERS * 2 * OWN))


def interp_matrix():
    distance = np.arange(ANGLES)[:, None] / 2 - 0.25 - np.arange(ANGLES // 2)[None, :]
    taper = np.where(np.abs(distance) < 4.0, 0.5 + 0.5 * np.cos(math.pi * distance / 4.0), 0.0)
    return bf16(np.sinc(distance) * taper).astype(np.float64)


def turned(rows, member):
    sign = 1 - 2 * member
    return np.exp(sign * 1j * TWO_PI * (2 * rows + 1) / 16)[:, None] / math.sqrt(2.0)


def merge_matrices():
    interp = interp_matrix()
    rows = np.arange(ANGLES)
    half = ANGLES // 2
    early = []
    for kind in range(4):
        second = slice(half * (kind % 2), half * (kind % 2) + half)
        first = slice(half * (kind // 2), half * (kind // 2) + half)
        blocks = []
        for late in range(2):
            for soon in range(2):
                two = (turned(rows, late) * interp)[second]
                one = (turned(rows, soon) * interp)[first]
                window = (two @ one)[:, STARTS[kind] : STARTS[kind] + WIDTHS[kind]]
                columns = complex_rows(window).reshape(2 * half, 2, -1).transpose(0, 2, 1)
                columns = columns.reshape(2 * half, -1)
                blocks.append(np.pad(columns, ((0, 0), (0, ROWS - columns.shape[1]))))
        early.append(np.concatenate(blocks, axis=1))
    last = [complex_rows(turned(rows, member) * interp) for member in range(2)]
    return bf16(np.stack(early)), bf16(np.concatenate(last, axis=1))


def bits(value):
    return lax.rem(value, 2), lax.rem(lax.div(value, 2), 2), lax.div(value, 4)


def swapped_bits(value):
    low, middle, high = bits(value)
    return low * 4 + middle * 2 + high


def kernel(
    delays,
    raw_in,
    dft_in,
    dft_half_in,
    twiddle_in,
    last_in,
    steer_in,
    early_in,
    image,
    raw,
    dft,
    dft_half,
    twiddle,
    last,
    steer,
    early,
    spread,
    packed,
    twisted,
    rolled,
    blocks,
    pulses,
    outgoing,
    incoming,
    ready,
    table_sem,
    plane_send,
    plane_recv,
    ring_send,
    ring_recv,
):
    sub = lax.axis_index("sub")
    gate = lax.axis_index("gate")
    half = lax.div(gate, PEERS)
    peer = lax.rem(gate, PEERS)
    place = half * N_SUB + sub
    sector = swapped_bits(sub)

    loads = [
        pltpu.make_async_copy(source, target, table_sem.at[i])
        for i, (source, target) in enumerate(
            (
                (raw_in, raw),
                (dft_in, dft),
                (twiddle_in, twiddle),
                (dft_half_in, dft_half),
                (steer_in.at[half], steer),
                (early_in.at[lax.rem(sector, 4)], early),
                (last_in, last),
            )
        )
    ]
    for load in loads:
        load.start()

    barrier = pltpu.get_barrier_semaphore()

    def at(spot):
        return {"sub": lax.rem(spot, N_SUB), "gate": lax.div(spot, N_SUB) * PEERS + peer}

    def greet_plane(step, carry):
        other = half * PEERS + lax.rem(peer + step, PEERS)
        pl.semaphore_signal(barrier, inc=1, device_id={"gate": other}, device_id_type=MESH)
        return carry

    def greet_ring(spot, carry):
        pl.semaphore_signal(barrier, inc=1, device_id=at(spot), device_id_type=MESH)
        return carry

    def answer_ring(spot, carry):
        pl.semaphore_signal(ready.at[place], inc=1, device_id=at(spot), device_id_type=MESH)
        return carry

    lax.fori_loop(1, PEERS, greet_plane, 0)
    lax.fori_loop(place + 1, RING, greet_ring, 0)

    for load in loads[:3]:
        load.wait()

    for part in range(2):
        spread[part] = raw[part].astype(jnp.float32).reshape(RADIX * OWN, RADIX)
    for part in range(2):
        for pulse in range(OWN):
            packed[part * RADIX : (part + 1) * RADIX, pulse * RADIX : (pulse + 1) * RADIX] = spread[
                part, pl.ds(pulse, RADIX, stride=OWN), :
            ].astype(jnp.bfloat16)
    cosine = twiddle[0]
    sine = twiddle[1]
    for pair in range(OWN // 2):
        section = jnp.dot(
            dft[...],
            packed[:, pair * 2 * RADIX : (pair + 1) * 2 * RADIX],
            preferred_element_type=jnp.float32,
        )
        for side in range(2):
            real = section[:RADIX, side * RADIX : (side + 1) * RADIX]
            imag = section[RADIX:, side * RADIX : (side + 1) * RADIX]
            rows = slice((2 * pair + side) * RADIX, (2 * pair + side + 1) * RADIX)
            twisted[rows, :RADIX] = (real * cosine - imag * sine).astype(jnp.bfloat16)
            twisted[rows, RADIX:] = (real * sine + imag * cosine).astype(jnp.bfloat16)
    lane = lax.broadcasted_iota(jnp.int32, (RADIX // HALVES, RADIX), 1)
    upper = lax.broadcasted_iota(jnp.int32, (8, RADIX), 0) < 4

    def range_gates(side):
        count = RADIX // HALVES
        for pair in range(OWN // 2):
            spectrum = lax.dot_general(
                dft_half[side],
                twisted[pair * 2 * RADIX : (pair + 1) * 2 * RADIX, :],
                (((1,), (1,)), ((), ())),
                preferred_element_type=jnp.float32,
            )
            for late in range(2):
                pulse = 2 * pair + late
                delay = delays[pulse]
                near = lane < RADIX - delay
                for part in range(2):
                    own = pltpu.roll(
                        spectrum[
                            part * HELD : (part + 1) * HELD, late * RADIX : (late + 1) * RADIX
                        ],
                        RADIX - delay,
                        1,
                    )
                    rolled[part, :, :] = own
                    after = rolled[part, 1 : count + 1, :]
                    spread[part, pl.ds(pulse, count, stride=OWN), :] = jnp.where(
                        near, own[:count], after
                    )
        rows = jnp.concatenate(
            [spread[part, : count * OWN].reshape(count, OWN, RADIX) for part in range(2)], axis=1
        ).astype(jnp.bfloat16)
        rows = rows.reshape(PEERS, 2, 2 * OWN, RADIX)
        for late in range(2):
            blocks[side, :, :, late * RADIX : (late + 1) * RADIX] = rows[:, late]

    def plane_copy(side, step):
        other = lax.rem(peer + step, PEERS)
        return pltpu.make_async_remote_copy(
            src_ref=blocks.at[side, other],
            dst_ref=pulses.at[side, peer],
            send_sem=plane_send.at[side],
            recv_sem=plane_recv.at[side],
            device_id={"gate": half * PEERS + other},
            device_id_type=MESH,
        )

    def plane_starts(side):
        def start(step, carry):
            plane_copy(side, step).start()
            return carry

        lax.fori_loop(1, PEERS, start, 0)
        pulses[side, peer] = blocks[side, peer]

    def plane_waits(side):
        others = pl.ds(0, PEERS - 1)
        pltpu.make_async_copy(
            blocks.at[side, others], pulses.at[side, others], plane_recv.at[side]
        ).wait()

    def beam_sums(side):
        beams = jnp.dot(
            steer[...],
            pulses[side].reshape(PEERS * 2 * OWN, BLOCK),
            preferred_element_type=jnp.float32,
        )
        for q in range(N_SUB):
            window = beams[q * ROWS : (q + 1) * ROWS].reshape(ROWS // 8, 8, BLOCK)
            shared = WIDTHS[q % 4] // 4
            base = (side * N_SUB + q) * TILES
            for t in range(shared):
                for lanes in range(2):
                    outgoing[base + 2 * t + lanes] = window[
                        t, :, lanes * RADIX : (lanes + 1) * RADIX
                    ].astype(jnp.bfloat16)
            outgoing[base + 2 * shared] = jnp.where(
                upper, window[shared, :, :RADIX], pltpu.roll(window[shared, :, RADIX:], 4, 0)
            ).astype(jnp.bfloat16)

    def ring_copy(spot, tiles):
        there = lax.rem(spot, N_SUB)
        source = (spot - there + swapped_bits(there)) * TILES
        return pltpu.make_async_remote_copy(
            src_ref=outgoing.at[pl.ds(source, tiles)],
            dst_ref=incoming.at[pl.ds(place * TILES, tiles)],
            send_sem=ring_send,
            recv_sem=ring_recv.at[lax.div(sub, 4)],
            device_id=at(spot),
            device_id_type=MESH,
        )

    def own_copy(tiles):
        return pltpu.make_async_copy(
            outgoing.at[pl.ds((half * N_SUB + sector) * TILES, tiles)],
            incoming.at[pl.ds(place * TILES, tiles)],
            ring_recv.at[lax.div(sub, 4)],
        )

    def on_edge(there):
        _, middle, high = bits(there)
        return middle == high

    def by_size(there, act):
        edge = on_edge(there)

        @pl.when(edge)
        def _():
            act(EDGE_TILES)

        @pl.when(jnp.logical_not(edge))
        def _():
            act(TILES)

    def ring_starts(side):
        def start(spot, carry):
            by_size(lax.rem(spot, N_SUB), lambda tiles: ring_copy(spot, tiles).start())
            return carry

        def start_later(spot, carry):
            pl.semaphore_wait(ready.at[spot], 1)
            return start(spot, carry)

        first = side * N_SUB
        lax.fori_loop(first, jnp.minimum(place, first + N_SUB), start, 0)
        lax.fori_loop(jnp.maximum(place + 1, first), first + N_SUB, start_later, 0)

    loads[3].wait()
    range_gates(0)
    pl.semaphore_wait(barrier, PEERS - 1 + place)
    plane_starts(0)
    lax.fori_loop(0, place, answer_ring, 0)
    range_gates(1)
    plane_starts(1)
    loads[4].wait()
    for side in range(HALVES):
        plane_waits(side)
        beam_sums(side)
        ring_starts(side)
    by_size(sub, lambda tiles: own_copy(tiles).start())
    for load in loads[5:]:
        load.wait()

    position = (
        gate * BLOCK + lax.broadcasted_iota(jnp.int32, (1, BLOCK), 1) + SAMPLES
    ).astype(jnp.float32)
    phase = (-TWO_PI * 84.0) / position
    gate_cos = jnp.cos(phase)
    gate_sin = jnp.sin(phase)

    edge = on_edge(sub)

    def taken(late, tiles):
        count = pl.ds(0, N_SUB * tiles)
        pltpu.make_async_copy(outgoing.at[count], incoming.at[count], ring_recv.at[late]).wait()

    total = None
    for late in range(2):
        by_size(sub, functools.partial(taken, late))
        children = []
        for s in range(4 * late, 4 * late + 4):
            both = [
                incoming[pl.ds((side * N_SUB + s) * TILES, TILES)].astype(jnp.float32)
                for side in range(HALVES)
            ]
            both = both[0] + both[1]
            paired = both[: TILES - 1].reshape(TILES // 2, 2, 8, RADIX)
            lanes = []
            for side in range(2):
                last_tile = both[TILES - 1]
                edge_tile = both[EDGE_TILES - 1]
                if side == 1:
                    last_tile = pltpu.roll(last_tile, 4, 0)
                    edge_tile = pltpu.roll(edge_tile, 4, 0)
                tiles = [
                    paired[: TILES // 2 - 1, side],
                    jnp.where(edge, edge_tile, paired[TILES // 2 - 1, side])[None],
                    jnp.where(edge, 0.0, last_tile)[None],
                ]
                lanes.append(jnp.concatenate(tiles, axis=0).reshape(ROWS, RADIX))
            children.append(jnp.concatenate(lanes, axis=1).astype(jnp.bfloat16))
        level_two = jnp.dot(
            early[...], jnp.concatenate(children, axis=0), preferred_element_type=jnp.float32
        ).astype(jnp.bfloat16)
        made = jnp.dot(
            last[:, late * ANGLES : (late + 1) * ANGLES],
            level_two,
            preferred_element_type=jnp.float32,
        )
        total = made if total is None else total + made
    real = total[:ANGLES]
    imag = total[ANGLES:]
    image[0] = (real * gate_cos - imag * gate_sin).astype(jnp.bfloat16)
    image[1] = (real * gate_sin + imag * gate_cos).astype(jnp.bfloat16)

    for side in range(HALVES):
        others = pl.ds(0, PEERS - 1)
        pltpu.make_async_copy(
            blocks.at[side, others], pulses.at[side, others], plane_send.at[side]
        ).wait()

    def sent(tiles):
        count = pl.ds(0, ALL_TILES - tiles)
        pltpu.make_async_copy(outgoing.at[count], incoming.at[count], ring_send).wait()

    by_size(sub, sent)


def per_device(raw_echo, delays):
    raw = raw_echo.reshape(2, OWN, RADIX, RADIX).transpose(0, 2, 1, 3)
    early, last = merge_matrices()
    dft, dft_half = dft_matrices()
    vmem = pl.BlockSpec(memory_space=pltpu.VMEM)
    hbm = pl.BlockSpec(memory_space=pl.ANY)
    return pl.pallas_call(
        kernel,
        out_shape=pltpu.VMEM((2, ANGLES, BLOCK), jnp.bfloat16),
        in_specs=[pl.BlockSpec(memory_space=pltpu.SMEM)] + [hbm] * 7,
        out_specs=vmem,
        scratch_shapes=[
            pltpu.VMEM((2, RADIX, OWN, RADIX), jnp.bfloat16),
            pltpu.VMEM(dft.shape, jnp.bfloat16),
            pltpu.VMEM(dft_half.shape, jnp.bfloat16),
            pltpu.VMEM((2, RADIX, RADIX), jnp.float32),
            pltpu.VMEM(last.shape, jnp.bfloat16),
            pltpu.VMEM((N_SUB * ROWS, PEERS * 2 * OWN), jnp.bfloat16),
            pltpu.VMEM((ANGLES, 4 * ROWS), jnp.bfloat16),
            pltpu.VMEM((2, RADIX * OWN, RADIX), jnp.float32),
            pltpu.VMEM((2 * RADIX, OWN * RADIX), jnp.bfloat16),
            pltpu.VMEM((OWN * RADIX, 2 * RADIX), jnp.bfloat16),
            pltpu.VMEM((2, HELD, RADIX), jnp.float32),
            pltpu.VMEM((HALVES, PEERS, 2 * OWN, BLOCK), jnp.bfloat16),
            pltpu.VMEM((HALVES, PEERS, 2 * OWN, BLOCK), jnp.bfloat16),
            pltpu.VMEM((RING * TILES, 8, RADIX), jnp.bfloat16),
            pltpu.VMEM((RING * TILES, 8, RADIX), jnp.bfloat16),
            pltpu.SemaphoreType.REGULAR((RING,)),
            pltpu.SemaphoreType.DMA((7,)),
            pltpu.SemaphoreType.DMA((HALVES,)),
            pltpu.SemaphoreType.DMA((HALVES,)),
            pltpu.SemaphoreType.DMA,
            pltpu.SemaphoreType.DMA((2,)),
        ],
        compiler_params=pltpu.CompilerParams(collective_id=0, has_side_effects=True),
        name="image_formation",
    )(
        delays,
        raw,
        jnp.asarray(dft),
        jnp.asarray(dft_half),
        jnp.asarray(twiddle_table()),
        jnp.asarray(last),
        jnp.asarray(steer_matrix()),
        jnp.asarray(early),
    )


def solution(mesh):
    placed = (P(None, ("sub", "gate"), None), P(("sub", "gate")))
    return jax.shard_map(
        per_device, mesh=mesh, in_specs=placed, out_specs=P(None, "sub", "gate"), check_vma=False
    )
```

```python
import functools
import math

import jax
import jax.numpy as jnp
import ml_dtypes
import numpy as np
from jax import lax
from jax.experimental import pallas as pl
from jax.experimental.pallas import tpu as pltpu
from jax.sharding import PartitionSpec as P

RADIX = 128
SAMPLES = 16384
ANGLES = 256
SUB_PULSES = 512
N_SUB = 8
HALVES = 2
PEERS = 32
RING = HALVES * N_SUB
STAGES = 3
OWN = 8
BLOCK = 256
WINDOW = 42
EDGE_WINDOW = 38
ROWS = 88
TILES = 21
EDGE_TILES = 19
FIRST_TILES = 10
ALL_TILES = N_SUB * (TILES + EDGE_TILES)
HELD = RADIX // HALVES + 8
STARTS = (0, 26, 60, 90)
WIDTHS = (EDGE_WINDOW, WINDOW, WINDOW, EDGE_WINDOW)
TWO_PI = 2.0 * math.pi
MESH = pl.DeviceIdType.MESH


def bf16(values):
    return values.astype(ml_dtypes.bfloat16)


def complex_rows(table):
    return np.block([[table.real, -table.imag], [table.imag, table.real]])


def dft_matrices():
    count = np.arange(RADIX)
    turns = (count[:, None] * count[None, :]) % RADIX
    table = np.exp(-1j * TWO_PI / RADIX * turns) / math.sqrt(RADIX)
    part = RADIX // HALVES
    rows = np.concatenate([table, np.zeros((8, RADIX))])
    halves = []
    for half in range(HALVES):
        own = rows[half * part : half * part + HELD].copy()
        own[part + 1 :] = 0
        halves.append(complex_rows(own))
    return bf16(complex_rows(table)), bf16(np.stack(halves))


def twiddle_table():
    count = np.arange(RADIX)
    turns = np.exp(-1j * TWO_PI / SAMPLES * (count[:, None] * count[None, :]))
    return np.stack([turns.real, turns.imag]).astype(np.float32)


def steer_matrix():
    result = np.zeros((HALVES, N_SUB, ROWS, PEERS * 2 * OWN))
    for half in range(HALVES):
        pulses = half * PEERS * OWN + np.arange(PEERS * OWN)
        for q in range(N_SUB):
            beams = 128 * (q // 4) + STARTS[q % 4] + np.arange(WIDTHS[q % 4])
            turns = (2 * beams[:, None] - ANGLES + 1) * (2 * pulses[None, :] - SUB_PULSES + 1)
            table = np.exp(-1j * TWO_PI / 4096 * (turns % 4096)) / math.sqrt(SUB_PULSES)
            table = table.reshape(-1, PEERS, OWN)
            upper = np.stack([table.real, -table.imag], axis=2)
            lower = np.stack([table.imag, table.real], axis=2)
            rows = np.stack([upper, lower], axis=1).reshape(-1, PEERS * 2 * OWN)
            result[half, q, : len(rows)] = rows
    return bf16(result.reshape(HALVES, N_SUB * ROWS, PEERS * 2 * OWN))


def interp_matrix():
    distance = np.arange(ANGLES)[:, None] / 2 - 0.25 - np.arange(ANGLES // 2)[None, :]
    taper = np.where(np.abs(distance) < 4.0, 0.5 + 0.5 * np.cos(math.pi * distance / 4.0), 0.0)
    return bf16(np.sinc(distance) * taper).astype(np.float64)


def turned(rows, member):
    sign = 1 - 2 * member
    return np.exp(sign * 1j * TWO_PI * (2 * rows + 1) / 16)[:, None] / math.sqrt(2.0)


def merge_matrices():
    interp = interp_matrix()
    rows = np.arange(ANGLES)
    half = ANGLES // 2
    early = []
    for kind in range(4):
        second = slice(half * (kind % 2), half * (kind % 2) + half)
        first = slice(half * (kind // 2), half * (kind // 2) + half)
        blocks = []
        for late in range(2):
            for soon in range(2):
                two = (turned(rows, late) * interp)[second]
                one = (turned(rows, soon) * interp)[first]
                window = (two @ one)[:, STARTS[kind] : STARTS[kind] + WIDTHS[kind]]
                columns = complex_rows(window).reshape(2 * half, 2, -1).transpose(0, 2, 1)
                columns = columns.reshape(2 * half, -1)
                blocks.append(np.pad(columns, ((0, 0), (0, ROWS - columns.shape[1]))))
        early.append(np.concatenate(blocks, axis=1))
    last = [complex_rows(turned(rows, member) * interp) for member in range(2)]
    return bf16(np.stack(early)), bf16(np.concatenate(last, axis=1))


def bits(value):
    return lax.rem(value, 2), lax.rem(lax.div(value, 2), 2), lax.div(value, 4)


def swapped_bits(value):
    low, middle, high = bits(value)
    return low * 4 + middle * 2 + high


def kernel(
    delays,
    raw_in,
    dft_in,
    dft_half_in,
    twiddle_in,
    last_in,
    steer_in,
    early_in,
    image,
    raw,
    dft,
    dft_half,
    twiddle,
    last,
    steer,
    early,
    spread,
    packed,
    twisted,
    rolled,
    blocks,
    pulses,
    kept,
    outgoing,
    incoming,
    ready,
    table_sem,
    plane_send,
    plane_recv,
    ring_send,
    ring_recv,
):
    sub = lax.axis_index("sub")
    gate = lax.axis_index("gate")
    half = lax.div(gate, PEERS)
    peer = lax.rem(gate, PEERS)
    place = half * N_SUB + sub
    sector = swapped_bits(sub)

    loads = [
        pltpu.make_async_copy(source, target, table_sem.at[i])
        for i, (source, target) in enumerate(
            (
                (raw_in, raw),
                (dft_in, dft),
                (twiddle_in, twiddle),
                (dft_half_in, dft_half),
                (steer_in.at[half], steer),
                (early_in.at[lax.rem(sector, 4)], early),
                (last_in, last),
            )
        )
    ]
    for load in loads:
        load.start()

    barrier = pltpu.get_barrier_semaphore()

    def at(spot):
        return {"sub": lax.rem(spot, N_SUB), "gate": lax.div(spot, N_SUB) * PEERS + peer}

    def greet_plane(step, carry):
        other = half * PEERS + lax.rem(peer + step, PEERS)
        pl.semaphore_signal(barrier, inc=1, device_id={"gate": other}, device_id_type=MESH)
        return carry

    def greet_ring(spot, carry):
        pl.semaphore_signal(barrier, inc=1, device_id=at(spot), device_id_type=MESH)
        return carry

    def answer_ring(spot, carry):
        pl.semaphore_signal(ready.at[place], inc=1, device_id=at(spot), device_id_type=MESH)
        return carry

    lax.fori_loop(1, PEERS, greet_plane, 0)
    lax.fori_loop(place + 1, RING, greet_ring, 0)

    for load in loads[:3]:
        load.wait()

    for part in range(2):
        spread[part] = raw[part].astype(jnp.float32).reshape(RADIX * OWN, RADIX)
    for part in range(2):
        for pulse in range(OWN):
            packed[part * RADIX : (part + 1) * RADIX, pulse * RADIX : (pulse + 1) * RADIX] = spread[
                part, pl.ds(pulse, RADIX, stride=OWN), :
            ].astype(jnp.bfloat16)
    cosine = twiddle[0]
    sine = twiddle[1]
    for pair in range(OWN // 2):
        section = jnp.dot(
            dft[...],
            packed[:, pair * 2 * RADIX : (pair + 1) * 2 * RADIX],
            preferred_element_type=jnp.float32,
        )
        for side in range(2):
            real = section[:RADIX, side * RADIX : (side + 1) * RADIX]
            imag = section[RADIX:, side * RADIX : (side + 1) * RADIX]
            rows = slice((2 * pair + side) * RADIX, (2 * pair + side + 1) * RADIX)
            twisted[rows, :RADIX] = (real * cosine - imag * sine).astype(jnp.bfloat16)
            twisted[rows, RADIX:] = (real * sine + imag * cosine).astype(jnp.bfloat16)
    lane = lax.broadcasted_iota(jnp.int32, (RADIX // HALVES, RADIX), 1)
    upper = lax.broadcasted_iota(jnp.int32, (8, RADIX), 0) < 4

    def range_gates(side):
        count = RADIX // HALVES
        for pair in range(OWN // 2):
            spectrum = lax.dot_general(
                dft_half[side],
                twisted[pair * 2 * RADIX : (pair + 1) * 2 * RADIX, :],
                (((1,), (1,)), ((), ())),
                preferred_element_type=jnp.float32,
            )
            for late in range(2):
                pulse = 2 * pair + late
                delay = delays[pulse]
                near = lane < RADIX - delay
                for part in range(2):
                    own = pltpu.roll(
                        spectrum[
                            part * HELD : (part + 1) * HELD, late * RADIX : (late + 1) * RADIX
                        ],
                        RADIX - delay,
                        1,
                    )
                    rolled[part, :, :] = own
                    after = rolled[part, 1 : count + 1, :]
                    spread[part, pl.ds(pulse, count, stride=OWN), :] = jnp.where(
                        near, own[:count], after
                    )
        rows = jnp.concatenate(
            [spread[part, : count * OWN].reshape(count, OWN, RADIX) for part in range(2)], axis=1
        ).astype(jnp.bfloat16)
        rows = rows.reshape(PEERS, 2, 2 * OWN, RADIX)
        for late in range(2):
            blocks[late, side] = rows[:, late]

    def lanes_of(stage):
        return pl.ds(stage, 1) if stage < 2 else pl.ds(0, 2)

    def plane_copy(stage, step):
        other = lax.rem(peer + step, PEERS)
        return pltpu.make_async_remote_copy(
            src_ref=blocks.at[lanes_of(stage), stage // 2, other],
            dst_ref=pulses.at[lanes_of(stage), stage // 2, peer],
            send_sem=plane_send.at[stage],
            recv_sem=plane_recv.at[stage],
            device_id={"gate": half * PEERS + other},
            device_id_type=MESH,
        )

    def plane_starts(stage):
        def start(step, carry):
            plane_copy(stage, step).start()
            return carry

        lax.fori_loop(1, PEERS, start, 0)
        for chunk in (stage,) if stage < 2 else (0, 1):
            pulses[chunk, stage // 2, peer] = blocks[chunk, stage // 2, peer]

    def plane_wait(stage, semaphores):
        others = pl.ds(0, PEERS - 1)
        pltpu.make_async_copy(
            blocks.at[lanes_of(stage), stage // 2, others],
            pulses.at[lanes_of(stage), stage // 2, others],
            semaphores.at[stage],
        ).wait()

    def beam_sums(stage):
        side = stage // 2
        chunks = (stage,) if stage < 2 else (0, 1)
        beams = jnp.dot(
            steer[...],
            jnp.concatenate(
                [pulses[chunk, side].reshape(PEERS * 2 * OWN, RADIX) for chunk in chunks], axis=1
            ),
            preferred_element_type=jnp.float32,
        )
        for place_in, chunk in enumerate(chunks):
            for q in range(N_SUB):
                window = beams[q * ROWS : (q + 1) * ROWS, place_in * RADIX : (place_in + 1) * RADIX]
                window = window.reshape(ROWS // 8, 8, RADIX)
                shared = WIDTHS[q % 4] // 4
                base = (side * N_SUB + q) * TILES + chunk * FIRST_TILES
                for t in range(shared):
                    outgoing[base + t] = window[t].astype(jnp.bfloat16)
                if chunk == 0:
                    kept[q] = window[shared]
                else:
                    outgoing[base + shared] = jnp.where(
                        upper, kept[q], pltpu.roll(window[shared], 4, 0)
                    ).astype(jnp.bfloat16)

    def ring_copy(chunk, spot, tiles):
        there = lax.rem(spot, N_SUB)
        source = (spot - there + swapped_bits(there)) * TILES + chunk * FIRST_TILES
        return pltpu.make_async_remote_copy(
            src_ref=outgoing.at[pl.ds(source, tiles)],
            dst_ref=incoming.at[pl.ds(place * TILES + chunk * FIRST_TILES, tiles)],
            send_sem=ring_send,
            recv_sem=ring_recv.at[lax.div(sub, 4)],
            device_id=at(spot),
            device_id_type=MESH,
        )

    def own_copy(chunk, tiles):
        source = (half * N_SUB + sector) * TILES + chunk * FIRST_TILES
        return pltpu.make_async_copy(
            outgoing.at[pl.ds(source, tiles)],
            incoming.at[pl.ds(place * TILES + chunk * FIRST_TILES, tiles)],
            ring_recv.at[lax.div(sub, 4)],
        )

    def on_edge(there):
        _, middle, high = bits(there)
        return middle == high

    def by_size(there, small, large, act):
        edge = on_edge(there)

        @pl.when(edge)
        def _():
            act(small)

        @pl.when(jnp.logical_not(edge))
        def _():
            act(large)

    def ring_starts(stage):
        side = stage // 2
        chunks = (stage,) if stage < 2 else (0, 1)

        def act(there, copy):
            def small(_):
                for chunk in chunks:
                    copy(chunk, EDGE_WINDOW // 4 + chunk).start()

            def large(_):
                for chunk in chunks:
                    copy(chunk, WINDOW // 4 + chunk).start()

            by_size(there, 0, 1, lambda size: (small, large)[size](None))

        def start(spot, carry):
            act(lax.rem(spot, N_SUB), lambda chunk, tiles: ring_copy(chunk, spot, tiles))
            return carry

        def start_later(spot, carry):
            if stage != 1:
                pl.semaphore_wait(ready.at[spot], 1)
            return start(spot, carry)

        first = side * N_SUB
        lax.fori_loop(first, jnp.minimum(place, first + N_SUB), start, 0)
        lax.fori_loop(jnp.maximum(place + 1, first), first + N_SUB, start_later, 0)

        @pl.when(half == side)
        def _():
            act(sub, own_copy)

    loads[3].wait()
    range_gates(0)
    pl.semaphore_wait(barrier, PEERS - 1 + place)
    lax.fori_loop(0, place, answer_ring, 0)
    plane_starts(0)
    plane_starts(1)
    range_gates(1)
    plane_starts(2)
    loads[4].wait()
    for stage in range(STAGES):
        plane_wait(stage, plane_recv)
        beam_sums(stage)
        ring_starts(stage)
    for load in loads[5:]:
        load.wait()

    position = (
        gate * BLOCK + lax.broadcasted_iota(jnp.int32, (1, BLOCK), 1) + SAMPLES
    ).astype(jnp.float32)
    phase = (-TWO_PI * 84.0) / position
    gate_cos = jnp.cos(phase)
    gate_sin = jnp.sin(phase)

    edge = on_edge(sub)

    def taken(late, tiles):
        count = pl.ds(0, N_SUB * tiles)
        pltpu.make_async_copy(outgoing.at[count], incoming.at[count], ring_recv.at[late]).wait()

    total = None
    for late in range(2):
        by_size(sub, EDGE_TILES, TILES, functools.partial(taken, late))
        children = []
        for s in range(4 * late, 4 * late + 4):
            both = [
                incoming[pl.ds((side * N_SUB + s) * TILES, TILES)].astype(jnp.float32)
                for side in range(HALVES)
            ]
            both = both[0] + both[1]
            lanes = []
            for chunk in range(2):
                ends = [both[EDGE_TILES], both[TILES - 1]]
                if chunk == 1:
                    ends = [pltpu.roll(end, 4, 0) for end in ends]
                first = chunk * FIRST_TILES
                tiles = [
                    both[first : first + FIRST_TILES - 1],
                    jnp.where(edge, ends[0], both[first + FIRST_TILES - 1])[None],
                    jnp.where(edge, 0.0, ends[1])[None],
                ]
                lanes.append(jnp.concatenate(tiles, axis=0).reshape(ROWS, RADIX))
            children.append(jnp.concatenate(lanes, axis=1).astype(jnp.bfloat16))
        level_two = jnp.dot(
            early[...], jnp.concatenate(children, axis=0), preferred_element_type=jnp.float32
        ).astype(jnp.bfloat16)
        made = jnp.dot(
            last[:, late * ANGLES : (late + 1) * ANGLES],
            level_two,
            preferred_element_type=jnp.float32,
        )
        total = made if total is None else total + made
    real = total[:ANGLES]
    imag = total[ANGLES:]
    image[0] = (real * gate_cos - imag * gate_sin).astype(jnp.bfloat16)
    image[1] = (real * gate_sin + imag * gate_cos).astype(jnp.bfloat16)

    for stage in range(STAGES):
        plane_wait(stage, plane_send)

    def sent(tiles):
        count = pl.ds(0, ALL_TILES - tiles)
        pltpu.make_async_copy(outgoing.at[count], incoming.at[count], ring_send).wait()

    by_size(sub, EDGE_TILES, TILES, sent)


def per_device(raw_echo, delays):
    raw = raw_echo.reshape(2, OWN, RADIX, RADIX).transpose(0, 2, 1, 3)
    early, last = merge_matrices()
    dft, dft_half = dft_matrices()
    vmem = pl.BlockSpec(memory_space=pltpu.VMEM)
    hbm = pl.BlockSpec(memory_space=pl.ANY)
    return pl.pallas_call(
        kernel,
        out_shape=pltpu.VMEM((2, ANGLES, BLOCK), jnp.bfloat16),
        in_specs=[pl.BlockSpec(memory_space=pltpu.SMEM)] + [hbm] * 7,
        out_specs=vmem,
        scratch_shapes=[
            pltpu.VMEM((2, RADIX, OWN, RADIX), jnp.bfloat16),
            pltpu.VMEM(dft.shape, jnp.bfloat16),
            pltpu.VMEM(dft_half.shape, jnp.bfloat16),
            pltpu.VMEM((2, RADIX, RADIX), jnp.float32),
            pltpu.VMEM(last.shape, jnp.bfloat16),
            pltpu.VMEM((N_SUB * ROWS, PEERS * 2 * OWN), jnp.bfloat16),
            pltpu.VMEM((ANGLES, 4 * ROWS), jnp.bfloat16),
            pltpu.VMEM((2, RADIX * OWN, RADIX), jnp.float32),
            pltpu.VMEM((2 * RADIX, OWN * RADIX), jnp.bfloat16),
            pltpu.VMEM((OWN * RADIX, 2 * RADIX), jnp.bfloat16),
            pltpu.VMEM((2, HELD, RADIX), jnp.float32),
            pltpu.VMEM((2, HALVES, PEERS, 2 * OWN, RADIX), jnp.bfloat16),
            pltpu.VMEM((2, HALVES, PEERS, 2 * OWN, RADIX), jnp.bfloat16),
            pltpu.VMEM((N_SUB, 8, RADIX), jnp.float32),
            pltpu.VMEM((RING * TILES, 8, RADIX), jnp.bfloat16),
            pltpu.VMEM((RING * TILES, 8, RADIX), jnp.bfloat16),
            pltpu.SemaphoreType.REGULAR((RING,)),
            pltpu.SemaphoreType.DMA((7,)),
            pltpu.SemaphoreType.DMA((STAGES,)),
            pltpu.SemaphoreType.DMA((STAGES,)),
            pltpu.SemaphoreType.DMA,
            pltpu.SemaphoreType.DMA((2,)),
        ],
        compiler_params=pltpu.CompilerParams(collective_id=0, has_side_effects=True),
        name="image_formation",
    )(
        delays,
        raw,
        jnp.asarray(dft),
        jnp.asarray(dft_half),
        jnp.asarray(twiddle_table()),
        jnp.asarray(last),
        jnp.asarray(steer_matrix()),
        jnp.asarray(early),
    )


def solution(mesh):
    placed = (P(None, ("sub", "gate"), None), P(("sub", "gate")))
    return jax.shard_map(
        per_device, mesh=mesh, in_specs=placed, out_specs=P(None, "sub", "gate"), check_vma=False
    )
```

```python
import functools
import math

import jax
import jax.numpy as jnp
import ml_dtypes
import numpy as np
from jax import lax
from jax.experimental import pallas as pl
from jax.experimental.pallas import tpu as pltpu
from jax.sharding import PartitionSpec as P

RADIX = 128
SAMPLES = 16384
ANGLES = 256
SUB_PULSES = 512
N_SUB = 8
HALVES = 2
PEERS = 32
RING = HALVES * N_SUB
STAGES = 3
OWN = 8
BLOCK = 256
WINDOW = 42
EDGE_WINDOW = 38
ROWS = 88
TILES = 21
EDGE_TILES = 19
FIRST_TILES = 10
ALL_TILES = N_SUB * (TILES + EDGE_TILES)
HELD = RADIX // HALVES + 8
STARTS = (0, 26, 60, 90)
WIDTHS = (EDGE_WINDOW, WINDOW, WINDOW, EDGE_WINDOW)
TWO_PI = 2.0 * math.pi
MESH = pl.DeviceIdType.MESH


def bf16(values):
    return values.astype(ml_dtypes.bfloat16)


def complex_rows(table):
    return np.block([[table.real, -table.imag], [table.imag, table.real]])


def dft_matrices():
    count = np.arange(RADIX)
    turns = (count[:, None] * count[None, :]) % RADIX
    table = np.exp(-1j * TWO_PI / RADIX * turns) / math.sqrt(RADIX)
    part = RADIX // HALVES
    rows = np.concatenate([table, np.zeros((8, RADIX))])
    halves = []
    for half in range(HALVES):
        own = rows[half * part : half * part + HELD].copy()
        own[part + 1 :] = 0
        halves.append(complex_rows(own))
    return bf16(complex_rows(table)), bf16(np.stack(halves))


def twiddle_table():
    count = np.arange(RADIX)
    turns = np.exp(-1j * TWO_PI / SAMPLES * (count[:, None] * count[None, :]))
    return np.stack([turns.real, turns.imag]).astype(np.float32)


def steer_matrix():
    result = np.zeros((HALVES, N_SUB, ROWS, PEERS * 2 * OWN))
    for half in range(HALVES):
        pulses = half * PEERS * OWN + np.arange(PEERS * OWN)
        for q in range(N_SUB):
            beams = 128 * (q // 4) + STARTS[q % 4] + np.arange(WIDTHS[q % 4])
            turns = (2 * beams[:, None] - ANGLES + 1) * (2 * pulses[None, :] - SUB_PULSES + 1)
            table = np.exp(-1j * TWO_PI / 4096 * (turns % 4096)) / math.sqrt(SUB_PULSES)
            table = table.reshape(-1, PEERS, OWN)
            upper = np.stack([table.real, -table.imag], axis=2)
            lower = np.stack([table.imag, table.real], axis=2)
            rows = np.stack([upper, lower], axis=1).reshape(-1, PEERS * 2 * OWN)
            result[half, q, : len(rows)] = rows
    return bf16(result.reshape(HALVES, N_SUB * ROWS, PEERS * 2 * OWN))


def interp_matrix():
    distance = np.arange(ANGLES)[:, None] / 2 - 0.25 - np.arange(ANGLES // 2)[None, :]
    taper = np.where(np.abs(distance) < 4.0, 0.5 + 0.5 * np.cos(math.pi * distance / 4.0), 0.0)
    return bf16(np.sinc(distance) * taper).astype(np.float64)


def turned(rows, member):
    sign = 1 - 2 * member
    return np.exp(sign * 1j * TWO_PI * (2 * rows + 1) / 16)[:, None] / math.sqrt(2.0)


def merge_matrices():
    interp = interp_matrix()
    rows = np.arange(ANGLES)
    half = ANGLES // 2
    early = []
    for kind in range(4):
        second = slice(half * (kind % 2), half * (kind % 2) + half)
        first = slice(half * (kind // 2), half * (kind // 2) + half)
        blocks = []
        for late in range(2):
            for soon in range(2):
                two = (turned(rows, late) * interp)[second]
                one = (turned(rows, soon) * interp)[first]
                window = (two @ one)[:, STARTS[kind] : STARTS[kind] + WIDTHS[kind]]
                columns = complex_rows(window).reshape(2 * half, 2, -1).transpose(0, 2, 1)
                columns = columns.reshape(2 * half, -1)
                blocks.append(np.pad(columns, ((0, 0), (0, ROWS - columns.shape[1]))))
        early.append(np.concatenate(blocks, axis=1))
    last = [complex_rows(turned(rows, member) * interp) for member in range(2)]
    return bf16(np.stack(early)), bf16(np.concatenate(last, axis=1))


def bits(value):
    return lax.rem(value, 2), lax.rem(lax.div(value, 2), 2), lax.div(value, 4)


def swapped_bits(value):
    low, middle, high = bits(value)
    return low * 4 + middle * 2 + high


def kernel(
    delays,
    raw_in,
    dft_in,
    dft_half_in,
    twiddle_in,
    last_in,
    steer_in,
    early_in,
    image,
    raw,
    dft,
    dft_half,
    twiddle,
    last,
    steer,
    early,
    spread,
    packed,
    twisted,
    rolled,
    blocks,
    pulses,
    kept,
    outgoing,
    incoming,
    ready,
    told,
    table_sem,
    plane_send,
    plane_recv,
    ring_send,
    ring_recv,
):
    sub = lax.axis_index("sub")
    gate = lax.axis_index("gate")
    half = lax.div(gate, PEERS)
    peer = lax.rem(gate, PEERS)
    place = half * N_SUB + sub
    core = lax.rem(peer, 2)
    sibling = peer + 1 - 2 * core
    sector = swapped_bits(sub)

    loads = [
        pltpu.make_async_copy(source, target, table_sem.at[i])
        for i, (source, target) in enumerate(
            (
                (raw_in, raw),
                (dft_in, dft),
                (twiddle_in, twiddle),
                (dft_half_in, dft_half),
                (steer_in.at[half], steer),
                (early_in.at[lax.rem(sector, 4)], early),
                (last_in, last),
            )
        )
    ]
    for load in loads:
        load.start()

    barrier = pltpu.get_barrier_semaphore()

    def at(spot, who=peer):
        return {"sub": lax.rem(spot, N_SUB), "gate": lax.div(spot, N_SUB) * PEERS + who}

    def signal(semaphore, to):
        pl.semaphore_signal(semaphore, inc=1, device_id=to, device_id_type=MESH)

    def greet_plane(step, carry):
        signal(barrier, at(place, lax.rem(peer - core + 2 * step, PEERS)))
        return carry

    def greet_ring(spot, carry):
        signal(barrier, at(spot, peer - core + 1))
        return carry

    def answer_ring(spot, carry):
        signal(ready.at[place], at(spot, peer))
        signal(ready.at[place], at(spot, sibling))
        return carry

    def hear_ring():
        pl.semaphore_wait(barrier, 2 * place + 1)
        lax.fori_loop(0, place, answer_ring, 0)
        signal(told, at(place, sibling))

    signal(barrier, at(place, sibling))
    lax.fori_loop(place + 1, RING, greet_ring, 0)
    lax.fori_loop(1, PEERS // 2, greet_plane, 0)

    for load in loads[:3]:
        load.wait()
    prompt = place < N_SUB + N_SUB // 2

    @pl.when((core == 1) & prompt)
    def _():
        hear_ring()

    for part in range(2):
        spread[part] = raw[part].astype(jnp.float32).reshape(RADIX * OWN, RADIX)
    for part in range(2):
        for pulse in range(OWN):
            packed[part * RADIX : (part + 1) * RADIX, pulse * RADIX : (pulse + 1) * RADIX] = spread[
                part, pl.ds(pulse, RADIX, stride=OWN), :
            ].astype(jnp.bfloat16)
    cosine = twiddle[0]
    sine = twiddle[1]
    for pair in range(OWN // 2):
        section = jnp.dot(
            dft[...],
            packed[:, pair * 2 * RADIX : (pair + 1) * 2 * RADIX],
            preferred_element_type=jnp.float32,
        )
        for side in range(2):
            real = section[:RADIX, side * RADIX : (side + 1) * RADIX]
            imag = section[RADIX:, side * RADIX : (side + 1) * RADIX]
            rows = slice((2 * pair + side) * RADIX, (2 * pair + side + 1) * RADIX)
            twisted[rows, :RADIX] = (real * cosine - imag * sine).astype(jnp.bfloat16)
            twisted[rows, RADIX:] = (real * sine + imag * cosine).astype(jnp.bfloat16)
    lane = lax.broadcasted_iota(jnp.int32, (RADIX // HALVES, RADIX), 1)
    upper = lax.broadcasted_iota(jnp.int32, (8, RADIX), 0) < 4

    def range_gates(side):
        count = RADIX // HALVES
        for pair in range(OWN // 2):
            spectrum = lax.dot_general(
                dft_half[side],
                twisted[pair * 2 * RADIX : (pair + 1) * 2 * RADIX, :],
                (((1,), (1,)), ((), ())),
                preferred_element_type=jnp.float32,
            )
            for late in range(2):
                pulse = 2 * pair + late
                delay = delays[pulse]
                near = lane < RADIX - delay
                for part in range(2):
                    own = pltpu.roll(
                        spectrum[
                            part * HELD : (part + 1) * HELD, late * RADIX : (late + 1) * RADIX
                        ],
                        RADIX - delay,
                        1,
                    )
                    rolled[part, :, :] = own
                    after = rolled[part, 1 : count + 1, :]
                    spread[part, pl.ds(pulse, count, stride=OWN), :] = jnp.where(
                        near, own[:count], after
                    )
        rows = jnp.concatenate(
            [spread[part, : count * OWN].reshape(count, OWN, RADIX) for part in range(2)], axis=1
        ).astype(jnp.bfloat16)
        rows = rows.reshape(PEERS, 2, 2 * OWN, RADIX)
        for late in range(2):
            blocks[late, side] = rows[:, late]

    def lanes_of(stage):
        return pl.ds(stage, 1) if stage < 2 else pl.ds(0, 2)

    def plane_copy(stage, step):
        other = lax.rem(peer + step, PEERS)
        return pltpu.make_async_remote_copy(
            src_ref=blocks.at[lanes_of(stage), stage // 2, other],
            dst_ref=pulses.at[lanes_of(stage), stage // 2, peer],
            send_sem=plane_send.at[stage],
            recv_sem=plane_recv.at[stage],
            device_id={"gate": half * PEERS + other},
            device_id_type=MESH,
        )

    def plane_starts(stage):
        def start(step, carry):
            far_first = 1 + lax.rem(step + PEERS // 2 - 2, PEERS - 1)
            plane_copy(stage, far_first).start()
            return carry

        lax.fori_loop(0, PEERS - 1, start, 0)
        for chunk in (stage,) if stage < 2 else (0, 1):
            pulses[chunk, stage // 2, peer] = blocks[chunk, stage // 2, peer]

    def plane_wait(stage, semaphores):
        others = pl.ds(0, PEERS - 1)
        pltpu.make_async_copy(
            blocks.at[lanes_of(stage), stage // 2, others],
            pulses.at[lanes_of(stage), stage // 2, others],
            semaphores.at[stage],
        ).wait()

    def beam_sums(stage):
        side = stage // 2
        chunks = (stage,) if stage < 2 else (0, 1)
        beams = jnp.dot(
            steer[...],
            jnp.concatenate(
                [pulses[chunk, side].reshape(PEERS * 2 * OWN, RADIX) for chunk in chunks], axis=1
            ),
            preferred_element_type=jnp.float32,
        )
        for place_in, chunk in enumerate(chunks):
            for q in range(N_SUB):
                window = beams[q * ROWS : (q + 1) * ROWS, place_in * RADIX : (place_in + 1) * RADIX]
                window = window.reshape(ROWS // 8, 8, RADIX)
                shared = WIDTHS[q % 4] // 4
                base = (side * N_SUB + q) * TILES + chunk * FIRST_TILES
                for t in range(shared):
                    outgoing[base + t] = window[t].astype(jnp.bfloat16)
                if chunk == 0:
                    kept[q] = window[shared]
                else:
                    outgoing[base + shared] = jnp.where(
                        upper, kept[q], pltpu.roll(window[shared], 4, 0)
                    ).astype(jnp.bfloat16)

    def ring_copy(chunk, spot, tiles):
        there = lax.rem(spot, N_SUB)
        source = (spot - there + swapped_bits(there)) * TILES + chunk * FIRST_TILES
        return pltpu.make_async_remote_copy(
            src_ref=outgoing.at[pl.ds(source, tiles)],
            dst_ref=incoming.at[pl.ds(place * TILES + chunk * FIRST_TILES, tiles)],
            send_sem=ring_send,
            recv_sem=ring_recv.at[lax.div(sub, 4)],
            device_id=at(spot),
            device_id_type=MESH,
        )

    def own_copy(chunk, tiles):
        source = (half * N_SUB + sector) * TILES + chunk * FIRST_TILES
        return pltpu.make_async_copy(
            outgoing.at[pl.ds(source, tiles)],
            incoming.at[pl.ds(place * TILES + chunk * FIRST_TILES, tiles)],
            ring_recv.at[lax.div(sub, 4)],
        )

    def on_edge(there):
        _, middle, high = bits(there)
        return middle == high

    def by_size(there, small, large, act):
        edge = on_edge(there)

        @pl.when(edge)
        def _():
            act(small)

        @pl.when(jnp.logical_not(edge))
        def _():
            act(large)

    def ring_starts(stage):
        side = stage // 2
        chunks = (stage,) if stage < 2 else (0, 1)

        def act(there, copy):
            def small(_):
                for chunk in chunks:
                    copy(chunk, EDGE_WINDOW // 4 + chunk).start()

            def large(_):
                for chunk in chunks:
                    copy(chunk, WINDOW // 4 + chunk).start()

            by_size(there, 0, 1, lambda size: (small, large)[size](None))

        def start(spot, carry):
            act(lax.rem(spot, N_SUB), lambda chunk, tiles: ring_copy(chunk, spot, tiles))
            return carry

        def start_later(spot, carry):
            if stage != 1:
                pl.semaphore_wait(ready.at[spot], 1)
            return start(spot, carry)

        first = side * N_SUB
        lax.fori_loop(first, jnp.minimum(place, first + N_SUB), start, 0)
        lax.fori_loop(jnp.maximum(place + 1, first), first + N_SUB, start_later, 0)

        @pl.when(half == side)
        def _():
            act(sub, own_copy)

    loads[3].wait()
    range_gates(0)

    @pl.when(core == 0)
    def _():
        pl.semaphore_wait(barrier, PEERS - 1)
        signal(told, at(place, sibling))

    @pl.when((core == 1) & jnp.logical_not(prompt))
    def _():
        hear_ring()

    @pl.when(core == 1)
    def _():
        pl.semaphore_wait(told, 1)

    plane_starts(0)
    plane_starts(1)
    range_gates(1)
    plane_starts(2)
    loads[4].wait()
    for stage in range(STAGES):
        plane_wait(stage, plane_recv)
        beam_sums(stage)
        if stage == 0:

            @pl.when(core == 0)
            def _():
                pl.semaphore_wait(told, 1)

        ring_starts(stage)
    for load in loads[5:]:
        load.wait()

    position = (
        gate * BLOCK + lax.broadcasted_iota(jnp.int32, (1, BLOCK), 1) + SAMPLES
    ).astype(jnp.float32)
    phase = (-TWO_PI * 84.0) / position
    gate_cos = jnp.cos(phase)
    gate_sin = jnp.sin(phase)

    edge = on_edge(sub)

    def taken(late, tiles):
        count = pl.ds(0, N_SUB * tiles)
        pltpu.make_async_copy(outgoing.at[count], incoming.at[count], ring_recv.at[late]).wait()

    total = None
    for late in range(2):
        by_size(sub, EDGE_TILES, TILES, functools.partial(taken, late))
        children = []
        for s in range(4 * late, 4 * late + 4):
            both = [
                incoming[pl.ds((side * N_SUB + s) * TILES, TILES)].astype(jnp.float32)
                for side in range(HALVES)
            ]
            both = both[0] + both[1]
            lanes = []
            for chunk in range(2):
                ends = [both[EDGE_TILES], both[TILES - 1]]
                if chunk == 1:
                    ends = [pltpu.roll(end, 4, 0) for end in ends]
                first = chunk * FIRST_TILES
                tiles = [
                    both[first : first + FIRST_TILES - 1],
                    jnp.where(edge, ends[0], both[first + FIRST_TILES - 1])[None],
                    jnp.where(edge, 0.0, ends[1])[None],
                ]
                lanes.append(jnp.concatenate(tiles, axis=0).reshape(ROWS, RADIX))
            children.append(jnp.concatenate(lanes, axis=1).astype(jnp.bfloat16))
        level_two = jnp.dot(
            early[...], jnp.concatenate(children, axis=0), preferred_element_type=jnp.float32
        ).astype(jnp.bfloat16)
        made = jnp.dot(
            last[:, late * ANGLES : (late + 1) * ANGLES],
            level_two,
            preferred_element_type=jnp.float32,
        )
        total = made if total is None else total + made
    real = total[:ANGLES]
    imag = total[ANGLES:]
    image[0] = (real * gate_cos - imag * gate_sin).astype(jnp.bfloat16)
    image[1] = (real * gate_sin + imag * gate_cos).astype(jnp.bfloat16)

    for stage in range(STAGES):
        plane_wait(stage, plane_send)

    def sent(tiles):
        count = pl.ds(0, ALL_TILES - tiles)
        pltpu.make_async_copy(outgoing.at[count], incoming.at[count], ring_send).wait()

    by_size(sub, EDGE_TILES, TILES, sent)


def per_device(raw_echo, delays):
    raw = raw_echo.reshape(2, OWN, RADIX, RADIX).transpose(0, 2, 1, 3)
    early, last = merge_matrices()
    dft, dft_half = dft_matrices()
    vmem = pl.BlockSpec(memory_space=pltpu.VMEM)
    hbm = pl.BlockSpec(memory_space=pl.ANY)
    return pl.pallas_call(
        kernel,
        out_shape=pltpu.VMEM((2, ANGLES, BLOCK), jnp.bfloat16),
        in_specs=[pl.BlockSpec(memory_space=pltpu.SMEM)] + [hbm] * 7,
        out_specs=vmem,
        scratch_shapes=[
            pltpu.VMEM((2, RADIX, OWN, RADIX), jnp.bfloat16),
            pltpu.VMEM(dft.shape, jnp.bfloat16),
            pltpu.VMEM(dft_half.shape, jnp.bfloat16),
            pltpu.VMEM((2, RADIX, RADIX), jnp.float32),
            pltpu.VMEM(last.shape, jnp.bfloat16),
            pltpu.VMEM((N_SUB * ROWS, PEERS * 2 * OWN), jnp.bfloat16),
            pltpu.VMEM((ANGLES, 4 * ROWS), jnp.bfloat16),
            pltpu.VMEM((2, RADIX * OWN, RADIX), jnp.float32),
            pltpu.VMEM((2 * RADIX, OWN * RADIX), jnp.bfloat16),
            pltpu.VMEM((OWN * RADIX, 2 * RADIX), jnp.bfloat16),
            pltpu.VMEM((2, HELD, RADIX), jnp.float32),
            pltpu.VMEM((2, HALVES, PEERS, 2 * OWN, RADIX), jnp.bfloat16),
            pltpu.VMEM((2, HALVES, PEERS, 2 * OWN, RADIX), jnp.bfloat16),
            pltpu.VMEM((N_SUB, 8, RADIX), jnp.float32),
            pltpu.VMEM((RING * TILES, 8, RADIX), jnp.bfloat16),
            pltpu.VMEM((RING * TILES, 8, RADIX), jnp.bfloat16),
            pltpu.SemaphoreType.REGULAR((RING,)),
            pltpu.SemaphoreType.REGULAR,
            pltpu.SemaphoreType.DMA((7,)),
            pltpu.SemaphoreType.DMA((STAGES,)),
            pltpu.SemaphoreType.DMA((STAGES,)),
            pltpu.SemaphoreType.DMA,
            pltpu.SemaphoreType.DMA((2,)),
        ],
        compiler_params=pltpu.CompilerParams(collective_id=0, has_side_effects=True),
        name="image_formation",
    )(
        delays,
        raw,
        jnp.asarray(dft),
        jnp.asarray(dft_half),
        jnp.asarray(twiddle_table()),
        jnp.asarray(last),
        jnp.asarray(steer_matrix()),
        jnp.asarray(early),
    )


def solution(mesh):
    placed = (P(None, ("sub", "gate"), None), P(("sub", "gate")))
    return jax.shard_map(
        per_device, mesh=mesh, in_specs=placed, out_specs=P(None, "sub", "gate"), check_vma=False
    )
```

```python
import functools
import math

import jax
import jax.numpy as jnp
import ml_dtypes
import numpy as np
from jax import lax
from jax.experimental import pallas as pl
from jax.experimental.pallas import tpu as pltpu
from jax.sharding import PartitionSpec as P

RADIX = 128
SAMPLES = 16384
ANGLES = 256
SUB_PULSES = 512
N_SUB = 8
HALVES = 2
PEERS = 32
RING = HALVES * N_SUB
STAGES = 3
BATCH = 4
OWN = 8
BLOCK = 256
WINDOW = 42
EDGE_WINDOW = 38
ROWS = 88
TILES = 21
EDGE_TILES = 19
FIRST_TILES = 10
ALL_TILES = N_SUB * (TILES + EDGE_TILES)
HELD = RADIX // HALVES + 8
SECTORS = (0, 4, 2, 6, 1, 5, 3, 7)
STARTS = (0, 26, 60, 90)
WIDTHS = (EDGE_WINDOW, WINDOW, WINDOW, EDGE_WINDOW)
TWO_PI = 2.0 * math.pi
MESH = pl.DeviceIdType.MESH


def bf16(values):
    return values.astype(ml_dtypes.bfloat16)


def complex_rows(table):
    return np.block([[table.real, -table.imag], [table.imag, table.real]])


def dft_matrices():
    count = np.arange(RADIX)
    turns = (count[:, None] * count[None, :]) % RADIX
    table = np.exp(-1j * TWO_PI / RADIX * turns) / math.sqrt(RADIX)
    part = RADIX // HALVES
    rows = np.concatenate([table, np.zeros((8, RADIX))])
    halves = []
    for half in range(HALVES):
        own = rows[half * part : half * part + HELD].copy()
        own[part + 1 :] = 0
        halves.append(complex_rows(own))
    return bf16(complex_rows(table)), bf16(np.stack(halves))


def twiddle_table():
    count = np.arange(RADIX)
    turns = np.exp(-1j * TWO_PI / SAMPLES * (count[:, None] * count[None, :]))
    return np.stack([turns.real, turns.imag]).astype(np.float32)


def steer_matrix():
    result = np.zeros((HALVES, N_SUB, ROWS, PEERS * 2 * OWN))
    for half in range(HALVES):
        pulses = half * PEERS * OWN + np.arange(PEERS * OWN)
        for slot, q in enumerate(SECTORS):
            beams = 128 * (q // 4) + STARTS[q % 4] + np.arange(WIDTHS[q % 4])
            turns = (2 * beams[:, None] - ANGLES + 1) * (2 * pulses[None, :] - SUB_PULSES + 1)
            table = np.exp(-1j * TWO_PI / 4096 * (turns % 4096)) / math.sqrt(SUB_PULSES)
            table = table.reshape(-1, PEERS, OWN)
            upper = np.stack([table.real, -table.imag], axis=2)
            lower = np.stack([table.imag, table.real], axis=2)
            rows = np.stack([upper, lower], axis=1).reshape(-1, PEERS * 2 * OWN)
            result[half, slot, : len(rows)] = rows
    return bf16(result.reshape(HALVES, N_SUB * ROWS, PEERS * 2 * OWN))


def interp_matrix():
    distance = np.arange(ANGLES)[:, None] / 2 - 0.25 - np.arange(ANGLES // 2)[None, :]
    taper = np.where(np.abs(distance) < 4.0, 0.5 + 0.5 * np.cos(math.pi * distance / 4.0), 0.0)
    return bf16(np.sinc(distance) * taper).astype(np.float64)


def turned(rows, member):
    sign = 1 - 2 * member
    return np.exp(sign * 1j * TWO_PI * (2 * rows + 1) / 16)[:, None] / math.sqrt(2.0)


def merge_matrices():
    interp = interp_matrix()
    rows = np.arange(ANGLES)
    half = ANGLES // 2
    early = []
    for kind in range(4):
        second = slice(half * (kind % 2), half * (kind % 2) + half)
        first = slice(half * (kind // 2), half * (kind // 2) + half)
        blocks = []
        for late in range(2):
            for soon in range(2):
                two = (turned(rows, late) * interp)[second]
                one = (turned(rows, soon) * interp)[first]
                window = (two @ one)[:, STARTS[kind] : STARTS[kind] + WIDTHS[kind]]
                columns = complex_rows(window).reshape(2 * half, 2, -1).transpose(0, 2, 1)
                columns = columns.reshape(2 * half, -1)
                blocks.append(np.pad(columns, ((0, 0), (0, ROWS - columns.shape[1]))))
        early.append(np.concatenate(blocks, axis=1))
    last = [complex_rows(turned(rows, member) * interp) for member in range(2)]
    return bf16(np.stack(early)), bf16(np.concatenate(last, axis=1))


def bits(value):
    return lax.rem(value, 2), lax.rem(lax.div(value, 2), 2), lax.div(value, 4)


def swapped_bits(value):
    low, middle, high = bits(value)
    return low * 4 + middle * 2 + high


def kernel(
    delays,
    raw_in,
    dft_in,
    dft_half_in,
    twiddle_in,
    last_in,
    steer_in,
    early_in,
    image,
    raw,
    dft,
    dft_half,
    twiddle,
    last,
    steer,
    early,
    spread,
    packed,
    twisted,
    rolled,
    blocks,
    pulses,
    kept,
    outgoing,
    incoming,
    ready,
    told,
    table_sem,
    plane_send,
    plane_recv,
    ring_send,
    ring_recv,
):
    sub = lax.axis_index("sub")
    gate = lax.axis_index("gate")
    half = lax.div(gate, PEERS)
    peer = lax.rem(gate, PEERS)
    place = half * N_SUB + sub
    core = lax.rem(peer, 2)
    sibling = peer + 1 - 2 * core
    sector = swapped_bits(sub)

    loads = [
        pltpu.make_async_copy(source, target, table_sem.at[i])
        for i, (source, target) in enumerate(
            (
                (raw_in, raw),
                (dft_in, dft),
                (twiddle_in, twiddle),
                (dft_half_in, dft_half),
                (steer_in.at[half], steer),
                (early_in.at[lax.rem(sector, 4)], early),
                (last_in, last),
            )
        )
    ]
    for load in loads:
        load.start()

    barrier = pltpu.get_barrier_semaphore()

    def at(spot, who=peer):
        return {"sub": lax.rem(spot, N_SUB), "gate": lax.div(spot, N_SUB) * PEERS + who}

    def signal(semaphore, to):
        pl.semaphore_signal(semaphore, inc=1, device_id=to, device_id_type=MESH)

    def greet_plane(step, carry):
        signal(barrier, at(place, lax.rem(peer - core + 2 * step, PEERS)))
        return carry

    def greet_ring(spot, carry):
        signal(barrier, at(spot, peer - core + 1))
        return carry

    def answer_ring(spot, carry):
        signal(ready.at[place], at(spot, peer))
        signal(ready.at[place], at(spot, sibling))
        return carry

    def hear_ring():
        pl.semaphore_wait(barrier, 2 * place + 1)
        lax.fori_loop(0, place, answer_ring, 0)
        signal(told, at(place, sibling))

    signal(barrier, at(place, sibling))
    lax.fori_loop(place + 1, RING, greet_ring, 0)
    lax.fori_loop(1, PEERS // 2, greet_plane, 0)

    for load in loads[:3]:
        load.wait()
    prompt = place < N_SUB + N_SUB // 2

    @pl.when((core == 1) & prompt)
    def _():
        hear_ring()

    for part in range(2):
        spread[part] = raw[part].astype(jnp.float32).reshape(RADIX * OWN, RADIX)
    for part in range(2):
        for pulse in range(OWN):
            packed[part * RADIX : (part + 1) * RADIX, pulse * RADIX : (pulse + 1) * RADIX] = spread[
                part, pl.ds(pulse, RADIX, stride=OWN), :
            ].astype(jnp.bfloat16)
    cosine = twiddle[0]
    sine = twiddle[1]
    for pair in range(OWN // 2):
        section = jnp.dot(
            dft[...],
            packed[:, pair * 2 * RADIX : (pair + 1) * 2 * RADIX],
            preferred_element_type=jnp.float32,
        )
        for side in range(2):
            real = section[:RADIX, side * RADIX : (side + 1) * RADIX]
            imag = section[RADIX:, side * RADIX : (side + 1) * RADIX]
            rows = slice((2 * pair + side) * RADIX, (2 * pair + side + 1) * RADIX)
            twisted[rows, :RADIX] = (real * cosine - imag * sine).astype(jnp.bfloat16)
            twisted[rows, RADIX:] = (real * sine + imag * cosine).astype(jnp.bfloat16)
    lane = lax.broadcasted_iota(jnp.int32, (RADIX // HALVES, RADIX), 1)
    upper = lax.broadcasted_iota(jnp.int32, (8, RADIX), 0) < 4

    def range_gates(side):
        count = RADIX // HALVES
        for pair in range(OWN // 2):
            spectrum = lax.dot_general(
                dft_half[side],
                twisted[pair * 2 * RADIX : (pair + 1) * 2 * RADIX, :],
                (((1,), (1,)), ((), ())),
                preferred_element_type=jnp.float32,
            )
            for late in range(2):
                pulse = 2 * pair + late
                delay = delays[pulse]
                near = lane < RADIX - delay
                for part in range(2):
                    own = pltpu.roll(
                        spectrum[
                            part * HELD : (part + 1) * HELD, late * RADIX : (late + 1) * RADIX
                        ],
                        RADIX - delay,
                        1,
                    )
                    rolled[part, :, :] = own
                    after = rolled[part, 1 : count + 1, :]
                    spread[part, pl.ds(pulse, count, stride=OWN), :] = jnp.where(
                        near, own[:count], after
                    )
        rows = jnp.concatenate(
            [spread[part, : count * OWN].reshape(count, OWN, RADIX) for part in range(2)], axis=1
        ).astype(jnp.bfloat16)
        rows = rows.reshape(PEERS, 2, 2 * OWN, RADIX)
        for late in range(2):
            blocks[late, side] = rows[:, late]

    def lanes_of(stage):
        return pl.ds(stage, 1) if stage < 2 else pl.ds(0, 2)

    def plane_copy(stage, step):
        other = lax.rem(peer + step, PEERS)
        return pltpu.make_async_remote_copy(
            src_ref=blocks.at[lanes_of(stage), stage // 2, other],
            dst_ref=pulses.at[lanes_of(stage), stage // 2, peer],
            send_sem=plane_send.at[stage],
            recv_sem=plane_recv.at[stage],
            device_id={"gate": half * PEERS + other},
            device_id_type=MESH,
        )

    def plane_starts(stage):
        def start(step, carry):
            far_first = 1 + lax.rem(step + PEERS // 2 - 2, PEERS - 1)
            plane_copy(stage, far_first).start()
            return carry

        lax.fori_loop(0, PEERS - 1, start, 0)
        for chunk in (stage,) if stage < 2 else (0, 1):
            pulses[chunk, stage // 2, peer] = blocks[chunk, stage // 2, peer]

    def plane_wait(stage, semaphores):
        others = pl.ds(0, PEERS - 1)
        pltpu.make_async_copy(
            blocks.at[lanes_of(stage), stage // 2, others],
            pulses.at[lanes_of(stage), stage // 2, others],
            semaphores.at[stage],
        ).wait()

    def beam_sums(stage, batch):
        side = stage // 2
        chunks = (stage,) if stage < 2 else (0, 1)
        beams = jnp.dot(
            steer[batch * BATCH * ROWS : (batch + 1) * BATCH * ROWS, :],
            jnp.concatenate(
                [pulses[chunk, side].reshape(PEERS * 2 * OWN, RADIX) for chunk in chunks], axis=1
            ),
            preferred_element_type=jnp.float32,
        )
        for place_in, chunk in enumerate(chunks):
            for slot in range(BATCH):
                q = SECTORS[batch * BATCH + slot]
                window = beams[slot * ROWS : (slot + 1) * ROWS, place_in * RADIX : (place_in + 1) * RADIX]
                window = window.reshape(ROWS // 8, 8, RADIX)
                shared = WIDTHS[q % 4] // 4
                base = (side * N_SUB + q) * TILES + chunk * FIRST_TILES
                for t in range(shared):
                    outgoing[base + t] = window[t].astype(jnp.bfloat16)
                if chunk == 0:
                    kept[q] = window[shared]
                else:
                    outgoing[base + shared] = jnp.where(
                        upper, kept[q], pltpu.roll(window[shared], 4, 0)
                    ).astype(jnp.bfloat16)

    def ring_copy(chunk, spot, tiles):
        there = lax.rem(spot, N_SUB)
        source = (spot - there + swapped_bits(there)) * TILES + chunk * FIRST_TILES
        return pltpu.make_async_remote_copy(
            src_ref=outgoing.at[pl.ds(source, tiles)],
            dst_ref=incoming.at[pl.ds(place * TILES + chunk * FIRST_TILES, tiles)],
            send_sem=ring_send,
            recv_sem=ring_recv.at[lax.div(sub, 4)],
            device_id=at(spot),
            device_id_type=MESH,
        )

    def own_copy(chunk, tiles):
        source = (half * N_SUB + sector) * TILES + chunk * FIRST_TILES
        return pltpu.make_async_copy(
            outgoing.at[pl.ds(source, tiles)],
            incoming.at[pl.ds(place * TILES + chunk * FIRST_TILES, tiles)],
            ring_recv.at[lax.div(sub, 4)],
        )

    def on_edge(there):
        _, middle, high = bits(there)
        return middle == high

    def by_size(there, small, large, act):
        edge = on_edge(there)

        @pl.when(edge)
        def _():
            act(small)

        @pl.when(jnp.logical_not(edge))
        def _():
            act(large)

    def ring_starts(stage, batch):
        side = stage // 2
        chunks = (stage,) if stage < 2 else (0, 1)

        def act(there, copy):
            def small(_):
                for chunk in chunks:
                    copy(chunk, EDGE_WINDOW // 4 + chunk).start()

            def large(_):
                for chunk in chunks:
                    copy(chunk, WINDOW // 4 + chunk).start()

            by_size(there, 0, 1, lambda size: (small, large)[size](None))

        def start(spot, carry):
            act(lax.rem(spot, N_SUB), lambda chunk, tiles: ring_copy(chunk, spot, tiles))
            return carry

        def start_later(spot, carry):
            if stage != 1:
                pl.semaphore_wait(ready.at[spot], 1)
            return start(spot, carry)

        first = side * N_SUB + batch * BATCH
        lax.fori_loop(first, jnp.minimum(place, first + BATCH), start, 0)
        lax.fori_loop(jnp.maximum(place + 1, first), first + BATCH, start_later, 0)

        if batch == 1:

            @pl.when(half == side)
            def _():
                act(sub, own_copy)

    loads[3].wait()
    range_gates(0)

    @pl.when(core == 0)
    def _():
        pl.semaphore_wait(barrier, PEERS - 1)
        signal(told, at(place, sibling))

    @pl.when((core == 1) & jnp.logical_not(prompt))
    def _():
        hear_ring()

    @pl.when(core == 1)
    def _():
        pl.semaphore_wait(told, 1)

    plane_starts(0)
    plane_starts(1)
    range_gates(1)
    plane_starts(2)
    loads[4].wait()
    for stage in range(STAGES):
        plane_wait(stage, plane_recv)
        for batch in range(N_SUB // BATCH):
            beam_sums(stage, batch)
            if stage == 0 and batch == 0:

                @pl.when(core == 0)
                def _():
                    pl.semaphore_wait(told, 1)

            ring_starts(stage, batch)
    for load in loads[5:]:
        load.wait()

    position = (
        gate * BLOCK + lax.broadcasted_iota(jnp.int32, (1, BLOCK), 1) + SAMPLES
    ).astype(jnp.float32)
    phase = (-TWO_PI * 84.0) / position
    gate_cos = jnp.cos(phase)
    gate_sin = jnp.sin(phase)

    edge = on_edge(sub)

    def taken(late, tiles):
        count = pl.ds(0, N_SUB * tiles)
        pltpu.make_async_copy(outgoing.at[count], incoming.at[count], ring_recv.at[late]).wait()

    total = None
    for late in range(2):
        by_size(sub, EDGE_TILES, TILES, functools.partial(taken, late))
        children = []
        for s in range(4 * late, 4 * late + 4):
            both = [
                incoming[pl.ds((side * N_SUB + s) * TILES, TILES)].astype(jnp.float32)
                for side in range(HALVES)
            ]
            both = both[0] + both[1]
            lanes = []
            for chunk in range(2):
                ends = [both[EDGE_TILES], both[TILES - 1]]
                if chunk == 1:
                    ends = [pltpu.roll(end, 4, 0) for end in ends]
                first = chunk * FIRST_TILES
                tiles = [
                    both[first : first + FIRST_TILES - 1],
                    jnp.where(edge, ends[0], both[first + FIRST_TILES - 1])[None],
                    jnp.where(edge, 0.0, ends[1])[None],
                ]
                lanes.append(jnp.concatenate(tiles, axis=0).reshape(ROWS, RADIX))
            children.append(jnp.concatenate(lanes, axis=1).astype(jnp.bfloat16))
        level_two = jnp.dot(
            early[...], jnp.concatenate(children, axis=0), preferred_element_type=jnp.float32
        ).astype(jnp.bfloat16)
        made = jnp.dot(
            last[:, late * ANGLES : (late + 1) * ANGLES],
            level_two,
            preferred_element_type=jnp.float32,
        )
        total = made if total is None else total + made
    real = total[:ANGLES]
    imag = total[ANGLES:]
    image[0] = (real * gate_cos - imag * gate_sin).astype(jnp.bfloat16)
    image[1] = (real * gate_sin + imag * gate_cos).astype(jnp.bfloat16)

    for stage in range(STAGES):
        plane_wait(stage, plane_send)

    def sent(tiles):
        count = pl.ds(0, ALL_TILES - tiles)
        pltpu.make_async_copy(outgoing.at[count], incoming.at[count], ring_send).wait()

    by_size(sub, EDGE_TILES, TILES, sent)


def per_device(raw_echo, delays):
    raw = raw_echo.reshape(2, OWN, RADIX, RADIX).transpose(0, 2, 1, 3)
    early, last = merge_matrices()
    dft, dft_half = dft_matrices()
    vmem = pl.BlockSpec(memory_space=pltpu.VMEM)
    hbm = pl.BlockSpec(memory_space=pl.ANY)
    return pl.pallas_call(
        kernel,
        out_shape=pltpu.VMEM((2, ANGLES, BLOCK), jnp.bfloat16),
        in_specs=[pl.BlockSpec(memory_space=pltpu.SMEM)] + [hbm] * 7,
        out_specs=vmem,
        scratch_shapes=[
            pltpu.VMEM((2, RADIX, OWN, RADIX), jnp.bfloat16),
            pltpu.VMEM(dft.shape, jnp.bfloat16),
            pltpu.VMEM(dft_half.shape, jnp.bfloat16),
            pltpu.VMEM((2, RADIX, RADIX), jnp.float32),
            pltpu.VMEM(last.shape, jnp.bfloat16),
            pltpu.VMEM((N_SUB * ROWS, PEERS * 2 * OWN), jnp.bfloat16),
            pltpu.VMEM((ANGLES, 4 * ROWS), jnp.bfloat16),
            pltpu.VMEM((2, RADIX * OWN, RADIX), jnp.float32),
            pltpu.VMEM((2 * RADIX, OWN * RADIX), jnp.bfloat16),
            pltpu.VMEM((OWN * RADIX, 2 * RADIX), jnp.bfloat16),
            pltpu.VMEM((2, HELD, RADIX), jnp.float32),
            pltpu.VMEM((2, HALVES, PEERS, 2 * OWN, RADIX), jnp.bfloat16),
            pltpu.VMEM((2, HALVES, PEERS, 2 * OWN, RADIX), jnp.bfloat16),
            pltpu.VMEM((N_SUB, 8, RADIX), jnp.float32),
            pltpu.VMEM((RING * TILES, 8, RADIX), jnp.bfloat16),
            pltpu.VMEM((RING * TILES, 8, RADIX), jnp.bfloat16),
            pltpu.SemaphoreType.REGULAR((RING,)),
            pltpu.SemaphoreType.REGULAR,
            pltpu.SemaphoreType.DMA((7,)),
            pltpu.SemaphoreType.DMA((STAGES,)),
            pltpu.SemaphoreType.DMA((STAGES,)),
            pltpu.SemaphoreType.DMA,
            pltpu.SemaphoreType.DMA((2,)),
        ],
        compiler_params=pltpu.CompilerParams(collective_id=0, has_side_effects=True),
        name="image_formation",
    )(
        delays,
        raw,
        jnp.asarray(dft),
        jnp.asarray(dft_half),
        jnp.asarray(twiddle_table()),
        jnp.asarray(last),
        jnp.asarray(steer_matrix()),
        jnp.asarray(early),
    )


def solution(mesh):
    placed = (P(None, ("sub", "gate"), None), P(("sub", "gate")))
    return jax.shard_map(
        per_device, mesh=mesh, in_specs=placed, out_specs=P(None, "sub", "gate"), check_vma=False
    )
```

```python
import functools
import math

import jax
import jax.numpy as jnp
import ml_dtypes
import numpy as np
from jax import lax
from jax.experimental import pallas as pl
from jax.experimental.pallas import tpu as pltpu
from jax.sharding import PartitionSpec as P

RADIX = 128
SAMPLES = 16384
ANGLES = 256
SUB_PULSES = 512
N_SUB = 8
HALVES = 2
PEERS = 32
RING = HALVES * N_SUB
STAGES = 3
BATCH = 4
OWN = 8
BLOCK = 256
WINDOW = 42
EDGE_WINDOW = 38
ROWS = 88
TILES = 21
EDGE_TILES = 19
FIRST_TILES = 10
ALL_TILES = N_SUB * (TILES + EDGE_TILES)
HELD = RADIX // HALVES + 8
SECTORS = (0, 4, 2, 6, 1, 5, 3, 7)
STARTS = (0, 26, 60, 90)
WIDTHS = (EDGE_WINDOW, WINDOW, WINDOW, EDGE_WINDOW)
TWO_PI = 2.0 * math.pi
MESH = pl.DeviceIdType.MESH


def bf16(values):
    return values.astype(ml_dtypes.bfloat16)


def complex_rows(table):
    return np.block([[table.real, -table.imag], [table.imag, table.real]])


def dft_matrices():
    count = np.arange(RADIX)
    turns = (count[:, None] * count[None, :]) % RADIX
    table = np.exp(-1j * TWO_PI / RADIX * turns) / math.sqrt(RADIX)
    part = RADIX // HALVES
    rows = np.concatenate([table, np.zeros((8, RADIX))])
    halves = []
    for half in range(HALVES):
        own = rows[half * part : half * part + HELD].copy()
        own[part + 1 :] = 0
        halves.append(complex_rows(own))
    return bf16(complex_rows(table)), bf16(np.stack(halves))


def twiddle_table():
    count = np.arange(RADIX)
    turns = np.exp(-1j * TWO_PI / SAMPLES * (count[:, None] * count[None, :]))
    return np.stack([turns.real, turns.imag]).astype(np.float32)


def steer_matrix():
    result = np.zeros((HALVES, N_SUB, ROWS, PEERS * 2 * OWN))
    for half in range(HALVES):
        pulses = half * PEERS * OWN + np.arange(PEERS * OWN)
        for slot, q in enumerate(SECTORS):
            beams = 128 * (q // 4) + STARTS[q % 4] + np.arange(WIDTHS[q % 4])
            turns = (2 * beams[:, None] - ANGLES + 1) * (2 * pulses[None, :] - SUB_PULSES + 1)
            table = np.exp(-1j * TWO_PI / 4096 * (turns % 4096)) / math.sqrt(SUB_PULSES)
            table = table.reshape(-1, PEERS, OWN)
            upper = np.stack([table.real, -table.imag], axis=2)
            lower = np.stack([table.imag, table.real], axis=2)
            rows = np.stack([upper, lower], axis=1).reshape(-1, PEERS * 2 * OWN)
            result[half, slot, : len(rows)] = rows
    return bf16(result.reshape(HALVES, N_SUB * ROWS, PEERS * 2 * OWN))


def interp_matrix():
    distance = np.arange(ANGLES)[:, None] / 2 - 0.25 - np.arange(ANGLES // 2)[None, :]
    taper = np.where(np.abs(distance) < 4.0, 0.5 + 0.5 * np.cos(math.pi * distance / 4.0), 0.0)
    return bf16(np.sinc(distance) * taper).astype(np.float64)


def turned(rows, member):
    sign = 1 - 2 * member
    return np.exp(sign * 1j * TWO_PI * (2 * rows + 1) / 16)[:, None] / math.sqrt(2.0)


def merge_matrices():
    interp = interp_matrix()
    rows = np.arange(ANGLES)
    half = ANGLES // 2
    early = []
    for kind in range(4):
        second = slice(half * (kind % 2), half * (kind % 2) + half)
        first = slice(half * (kind // 2), half * (kind // 2) + half)
        blocks = []
        for late in range(2):
            for soon in range(2):
                two = (turned(rows, late) * interp)[second]
                one = (turned(rows, soon) * interp)[first]
                window = (two @ one)[:, STARTS[kind] : STARTS[kind] + WIDTHS[kind]]
                columns = complex_rows(window).reshape(2 * half, 2, -1).transpose(0, 2, 1)
                columns = columns.reshape(2 * half, -1)
                blocks.append(np.pad(columns, ((0, 0), (0, ROWS - columns.shape[1]))))
        early.append(np.concatenate(blocks, axis=1))
    last = [complex_rows(turned(rows, member) * interp) for member in range(2)]
    return bf16(np.stack(early)), bf16(np.concatenate(last, axis=1))


def bits(value):
    return lax.rem(value, 2), lax.rem(lax.div(value, 2), 2), lax.div(value, 4)


def swapped_bits(value):
    low, middle, high = bits(value)
    return low * 4 + middle * 2 + high


def kernel(
    delays,
    raw_in,
    dft_in,
    dft_half_in,
    twiddle_in,
    last_in,
    steer_in,
    early_in,
    image,
    raw,
    dft,
    dft_half,
    twiddle,
    last,
    steer,
    early,
    spread,
    packed,
    twisted,
    rolled,
    blocks,
    pulses,
    kept,
    outgoing,
    incoming,
    ready,
    told,
    table_sem,
    plane_send,
    plane_recv,
    ring_send,
    ring_recv,
):
    sub = lax.axis_index("sub")
    gate = lax.axis_index("gate")
    half = lax.div(gate, PEERS)
    peer = lax.rem(gate, PEERS)
    place = half * N_SUB + sub
    core = lax.rem(peer, 2)
    sibling = peer + 1 - 2 * core
    sector = swapped_bits(sub)

    loads = [
        pltpu.make_async_copy(source, target, table_sem.at[i])
        for i, (source, target) in enumerate(
            (
                (raw_in, raw),
                (dft_in, dft),
                (twiddle_in, twiddle),
                (dft_half_in, dft_half),
                (steer_in.at[half], steer),
                (early_in.at[lax.rem(sector, 4)], early),
                (last_in, last),
            )
        )
    ]
    for load in loads:
        load.start()

    barrier = pltpu.get_barrier_semaphore()

    def at(spot, who=peer):
        return {"sub": lax.rem(spot, N_SUB), "gate": lax.div(spot, N_SUB) * PEERS + who}

    def signal(semaphore, to):
        pl.semaphore_signal(semaphore, inc=1, device_id=to, device_id_type=MESH)

    def greet_plane(step, carry):
        signal(barrier, at(place, lax.rem(peer - core + 2 * step, PEERS)))
        return carry

    def greet_ring(spot, carry):
        signal(barrier, at(spot, peer - core + 1))
        return carry

    def answer_ring(spot, carry):
        signal(ready.at[place], at(spot, peer))
        signal(ready.at[place], at(spot, sibling))
        return carry

    def hear_ring():
        pl.semaphore_wait(barrier, 2 * place + 1)
        lax.fori_loop(0, place, answer_ring, 0)
        signal(told, at(place, sibling))

    signal(barrier, at(place, sibling))
    lax.fori_loop(place + 1, RING, greet_ring, 0)
    lax.fori_loop(1, PEERS // 2, greet_plane, 0)

    for load in loads[:3]:
        load.wait()
    prompt = place < N_SUB + N_SUB // 2

    @pl.when((core == 1) & prompt)
    def _():
        hear_ring()

    for part in range(2):
        spread[part] = raw[part].astype(jnp.float32).reshape(RADIX * OWN, RADIX)
    for part in range(2):
        for pulse in range(OWN):
            packed[part * RADIX : (part + 1) * RADIX, pulse * RADIX : (pulse + 1) * RADIX] = spread[
                part, pl.ds(pulse, RADIX, stride=OWN), :
            ].astype(jnp.bfloat16)
    cosine = twiddle[0]
    sine = twiddle[1]
    for pair in range(OWN // 2):
        section = jnp.dot(
            dft[...],
            packed[:, pair * 2 * RADIX : (pair + 1) * 2 * RADIX],
            preferred_element_type=jnp.float32,
        )
        for side in range(2):
            real = section[:RADIX, side * RADIX : (side + 1) * RADIX]
            imag = section[RADIX:, side * RADIX : (side + 1) * RADIX]
            rows = slice((2 * pair + side) * RADIX, (2 * pair + side + 1) * RADIX)
            twisted[rows, :RADIX] = (real * cosine - imag * sine).astype(jnp.bfloat16)
            twisted[rows, RADIX:] = (real * sine + imag * cosine).astype(jnp.bfloat16)
    lane = lax.broadcasted_iota(jnp.int32, (RADIX // HALVES, RADIX), 1)
    upper = lax.broadcasted_iota(jnp.int32, (8, RADIX), 0) < 4

    def range_gates(side):
        count = RADIX // HALVES
        for pair in range(OWN // 2):
            spectrum = lax.dot_general(
                dft_half[side],
                twisted[pair * 2 * RADIX : (pair + 1) * 2 * RADIX, :],
                (((1,), (1,)), ((), ())),
                preferred_element_type=jnp.float32,
            )
            for late in range(2):
                pulse = 2 * pair + late
                delay = delays[pulse]
                near = lane < RADIX - delay
                for part in range(2):
                    own = pltpu.roll(
                        spectrum[
                            part * HELD : (part + 1) * HELD, late * RADIX : (late + 1) * RADIX
                        ],
                        RADIX - delay,
                        1,
                    )
                    rolled[part, :, :] = own
                    after = rolled[part, 1 : count + 1, :]
                    spread[part, pl.ds(pulse, count, stride=OWN), :] = jnp.where(
                        near, own[:count], after
                    )
        rows = jnp.concatenate(
            [spread[part, : count * OWN].reshape(count, OWN, RADIX) for part in range(2)], axis=1
        ).astype(jnp.bfloat16)
        rows = rows.reshape(PEERS, 2, 2 * OWN, RADIX)
        for late in range(2):
            blocks[late, side] = rows[:, late]

    def lanes_of(stage):
        return pl.ds(stage, 1) if stage < 2 else pl.ds(0, 2)

    def plane_copy(stage, step):
        other = lax.rem(peer + step, PEERS)
        return pltpu.make_async_remote_copy(
            src_ref=blocks.at[lanes_of(stage), stage // 2, other],
            dst_ref=pulses.at[lanes_of(stage), stage // 2, peer],
            send_sem=plane_send.at[stage],
            recv_sem=plane_recv.at[stage],
            device_id={"gate": half * PEERS + other},
            device_id_type=MESH,
        )

    def plane_starts(stage):
        def start(step, carry):
            far_first = 1 + lax.rem(step + PEERS // 2 - 2, PEERS - 1)
            plane_copy(stage, far_first).start()
            return carry

        lax.fori_loop(0, PEERS - 1, start, 0)
        for chunk in (stage,) if stage < 2 else (0, 1):
            pulses[chunk, stage // 2, peer] = blocks[chunk, stage // 2, peer]

    def plane_wait(stage, semaphores):
        others = pl.ds(0, PEERS - 1)
        pltpu.make_async_copy(
            blocks.at[lanes_of(stage), stage // 2, others],
            pulses.at[lanes_of(stage), stage // 2, others],
            semaphores.at[stage],
        ).wait()

    def beam_sums(stage, batch):
        side = stage // 2
        chunks = (stage,) if stage < 2 else (0, 1)
        beams = jnp.dot(
            steer[batch * BATCH * ROWS : (batch + 1) * BATCH * ROWS, :],
            jnp.concatenate(
                [pulses[chunk, side].reshape(PEERS * 2 * OWN, RADIX) for chunk in chunks], axis=1
            ),
            preferred_element_type=jnp.float32,
        )
        for place_in, chunk in enumerate(chunks):
            for slot in range(BATCH):
                q = SECTORS[batch * BATCH + slot]
                window = beams[slot * ROWS : (slot + 1) * ROWS, place_in * RADIX : (place_in + 1) * RADIX]
                window = window.reshape(ROWS // 8, 8, RADIX)
                shared = WIDTHS[q % 4] // 4
                base = (side * N_SUB + q) * TILES + chunk * FIRST_TILES
                for t in range(shared):
                    outgoing[base + t] = window[t].astype(jnp.bfloat16)
                if chunk == 0:
                    kept[q] = window[shared]
                else:
                    outgoing[base + shared] = jnp.where(
                        upper, kept[q], pltpu.roll(window[shared], 4, 0)
                    ).astype(jnp.bfloat16)

    def ring_copy(chunk, spot, tiles):
        there = lax.rem(spot, N_SUB)
        source = (spot - there + swapped_bits(there)) * TILES + chunk * FIRST_TILES
        return pltpu.make_async_remote_copy(
            src_ref=outgoing.at[pl.ds(source, tiles)],
            dst_ref=incoming.at[pl.ds(place * TILES + chunk * FIRST_TILES, tiles)],
            send_sem=ring_send,
            recv_sem=ring_recv.at[lax.div(sub, 4)],
            device_id=at(spot),
            device_id_type=MESH,
        )

    def own_copy(chunk, tiles):
        source = (half * N_SUB + sector) * TILES + chunk * FIRST_TILES
        return pltpu.make_async_copy(
            outgoing.at[pl.ds(source, tiles)],
            incoming.at[pl.ds(place * TILES + chunk * FIRST_TILES, tiles)],
            ring_recv.at[lax.div(sub, 4)],
        )

    def on_edge(there):
        _, middle, high = bits(there)
        return middle == high

    def by_size(there, small, large, act):
        edge = on_edge(there)

        @pl.when(edge)
        def _():
            act(small)

        @pl.when(jnp.logical_not(edge))
        def _():
            act(large)

    def ring_starts(stage, batch):
        side = stage // 2
        chunks = (stage,) if stage < 2 else (0, 1)

        def act(there, copy):
            def small(_):
                for chunk in chunks:
                    copy(chunk, EDGE_WINDOW // 4 + chunk).start()

            def large(_):
                for chunk in chunks:
                    copy(chunk, WINDOW // 4 + chunk).start()

            by_size(there, 0, 1, lambda size: (small, large)[size](None))

        def start(spot, carry):
            act(lax.rem(spot, N_SUB), lambda chunk, tiles: ring_copy(chunk, spot, tiles))
            return carry

        def start_later(spot, carry):
            if stage != 1:
                pl.semaphore_wait(ready.at[spot], 1)
            return start(spot, carry)

        first = side * N_SUB + batch * BATCH
        lax.fori_loop(first, jnp.minimum(place, first + BATCH), start, 0)
        later = jnp.maximum(place + 1, first)
        stop = first + BATCH
        if stage == 2:
            lax.fori_loop(later, stop, lambda i, c: start_later(later + stop - 1 - i, c), 0)
        else:
            lax.fori_loop(later, stop, start_later, 0)

        if batch == (1 if stage < 2 else 0):

            @pl.when(half == side)
            def _():
                act(sub, own_copy)

    loads[3].wait()
    range_gates(0)

    @pl.when(core == 0)
    def _():
        pl.semaphore_wait(barrier, PEERS - 1)
        signal(told, at(place, sibling))

    @pl.when((core == 1) & jnp.logical_not(prompt))
    def _():
        hear_ring()

    @pl.when(core == 1)
    def _():
        pl.semaphore_wait(told, 1)

    plane_starts(0)
    plane_starts(1)
    range_gates(1)
    plane_starts(2)
    loads[4].wait()
    for stage in range(STAGES):
        plane_wait(stage, plane_recv)
        for batch in (0, 1) if stage < 2 else (1, 0):
            beam_sums(stage, batch)
            if stage == 0 and batch == 0:

                @pl.when(core == 0)
                def _():
                    pl.semaphore_wait(told, 1)

            ring_starts(stage, batch)
    for load in loads[5:]:
        load.wait()

    position = (
        gate * BLOCK + lax.broadcasted_iota(jnp.int32, (1, BLOCK), 1) + SAMPLES
    ).astype(jnp.float32)
    phase = (-TWO_PI * 84.0) / position
    gate_cos = jnp.cos(phase)
    gate_sin = jnp.sin(phase)

    edge = on_edge(sub)

    def taken(late, tiles):
        count = pl.ds(0, N_SUB * tiles)
        pltpu.make_async_copy(outgoing.at[count], incoming.at[count], ring_recv.at[late]).wait()

    total = None
    for late in range(2):
        by_size(sub, EDGE_TILES, TILES, functools.partial(taken, late))
        children = []
        for s in range(4 * late, 4 * late + 4):
            both = [
                incoming[pl.ds((side * N_SUB + s) * TILES, TILES)].astype(jnp.float32)
                for side in range(HALVES)
            ]
            both = both[0] + both[1]
            lanes = []
            for chunk in range(2):
                ends = [both[EDGE_TILES], both[TILES - 1]]
                if chunk == 1:
                    ends = [pltpu.roll(end, 4, 0) for end in ends]
                first = chunk * FIRST_TILES
                tiles = [
                    both[first : first + FIRST_TILES - 1],
                    jnp.where(edge, ends[0], both[first + FIRST_TILES - 1])[None],
                    jnp.where(edge, 0.0, ends[1])[None],
                ]
                lanes.append(jnp.concatenate(tiles, axis=0).reshape(ROWS, RADIX))
            children.append(jnp.concatenate(lanes, axis=1).astype(jnp.bfloat16))
        level_two = jnp.dot(
            early[...], jnp.concatenate(children, axis=0), preferred_element_type=jnp.float32
        ).astype(jnp.bfloat16)
        made = jnp.dot(
            last[:, late * ANGLES : (late + 1) * ANGLES],
            level_two,
            preferred_element_type=jnp.float32,
        )
        total = made if total is None else total + made
    real = total[:ANGLES]
    imag = total[ANGLES:]
    image[0] = (real * gate_cos - imag * gate_sin).astype(jnp.bfloat16)
    image[1] = (real * gate_sin + imag * gate_cos).astype(jnp.bfloat16)

    for stage in range(STAGES):
        plane_wait(stage, plane_send)

    def sent(tiles):
        count = pl.ds(0, ALL_TILES - tiles)
        pltpu.make_async_copy(outgoing.at[count], incoming.at[count], ring_send).wait()

    by_size(sub, EDGE_TILES, TILES, sent)


def per_device(raw_echo, delays):
    raw = raw_echo.reshape(2, OWN, RADIX, RADIX).transpose(0, 2, 1, 3)
    early, last = merge_matrices()
    dft, dft_half = dft_matrices()
    vmem = pl.BlockSpec(memory_space=pltpu.VMEM)
    hbm = pl.BlockSpec(memory_space=pl.ANY)
    return pl.pallas_call(
        kernel,
        out_shape=pltpu.VMEM((2, ANGLES, BLOCK), jnp.bfloat16),
        in_specs=[pl.BlockSpec(memory_space=pltpu.SMEM)] + [hbm] * 7,
        out_specs=vmem,
        scratch_shapes=[
            pltpu.VMEM((2, RADIX, OWN, RADIX), jnp.bfloat16),
            pltpu.VMEM(dft.shape, jnp.bfloat16),
            pltpu.VMEM(dft_half.shape, jnp.bfloat16),
            pltpu.VMEM((2, RADIX, RADIX), jnp.float32),
            pltpu.VMEM(last.shape, jnp.bfloat16),
            pltpu.VMEM((N_SUB * ROWS, PEERS * 2 * OWN), jnp.bfloat16),
            pltpu.VMEM((ANGLES, 4 * ROWS), jnp.bfloat16),
            pltpu.VMEM((2, RADIX * OWN, RADIX), jnp.float32),
            pltpu.VMEM((2 * RADIX, OWN * RADIX), jnp.bfloat16),
            pltpu.VMEM((OWN * RADIX, 2 * RADIX), jnp.bfloat16),
            pltpu.VMEM((2, HELD, RADIX), jnp.float32),
            pltpu.VMEM((2, HALVES, PEERS, 2 * OWN, RADIX), jnp.bfloat16),
            pltpu.VMEM((2, HALVES, PEERS, 2 * OWN, RADIX), jnp.bfloat16),
            pltpu.VMEM((N_SUB, 8, RADIX), jnp.float32),
            pltpu.VMEM((RING * TILES, 8, RADIX), jnp.bfloat16),
            pltpu.VMEM((RING * TILES, 8, RADIX), jnp.bfloat16),
            pltpu.SemaphoreType.REGULAR((RING,)),
            pltpu.SemaphoreType.REGULAR,
            pltpu.SemaphoreType.DMA((7,)),
            pltpu.SemaphoreType.DMA((STAGES,)),
            pltpu.SemaphoreType.DMA((STAGES,)),
            pltpu.SemaphoreType.DMA,
            pltpu.SemaphoreType.DMA((2,)),
        ],
        compiler_params=pltpu.CompilerParams(collective_id=0, has_side_effects=True),
        name="image_formation",
    )(
        delays,
        raw,
        jnp.asarray(dft),
        jnp.asarray(dft_half),
        jnp.asarray(twiddle_table()),
        jnp.asarray(last),
        jnp.asarray(steer_matrix()),
        jnp.asarray(early),
    )


def solution(mesh):
    placed = (P(None, ("sub", "gate"), None), P(("sub", "gate")))
    return jax.shard_map(
        per_device, mesh=mesh, in_specs=placed, out_specs=P(None, "sub", "gate"), check_vma=False
    )
```
